256 devices in a mesh: nodes: 64 (over x, z, core), mp: 4 (over y).
Axes of the slice: x: 4, y: 4, z: 8, core: 2. Of those that a mesh axis runs over, the one named last changes fastest.
Arguments:
- tokens: bfloat16 [2048, 64, 768], P('nodes'), may hold values from -32 to 32
- w_query: bfloat16 [768, 768], P('mp'), may hold values from -0.5 to 0.5
- w_key: bfloat16 [768, 768], P('mp'), may hold values from -0.5 to 0.5
- w_value: bfloat16 [768, 768], P('mp'), may hold values from -0.21875 to 0.21875
- grad_out: bfloat16 [2048, 12, 4096], P('nodes', 'mp'), may hold values from -6 to 6
- owned_cls: bfloat16 [768, 131072], P('mp', 'nodes'), may hold values from -24 to 24
- send_rows: int32 [64, 64, 32], P('nodes'), may hold values from 0 to 2047
- neigh_slot: int32 [2048, 2, 32], P('nodes'), may hold values from 0 to 2047
- neigh_count: int32 [2048, 2], P('nodes'), may hold values from 1 to 32
Outputs:
- context: bfloat16 [2048, 12, 4096], P('nodes', 'mp')
- grad_query: float32 [768, 768], P('mp')
- grad_key: float32 [768, 768], P('mp')
- grad_value: float32 [768, 768], P('mp')
- grad_cls: float32 [768, 131072], P('mp', 'nodes')
The draws below stay inside these ranges and needn't reach their ends.
Inputs may be any that keep to these rules, and one draw needn't show every extreme that they name: send_rows[o, r, :] are rows of owner o's own block; rows may repeat. `neigh_slot`: entries with k >= neigh_count[c, t] are not used.
All inputs are finite; a program needn't handle non-finite values.
Results may differ from the reference program's by a relative error of at most 0.012.
The reference program's roundings to bfloat16 on the way (of `fetched`, `virtual`, `key_input`, `probs_low`, `value_grads` and `score_grads`) count: a program that leaves them out, or rounds other values in their place, can miss the bound.
Values may be sent and summed in bfloat16 or wider, within the bound.
No kernel may reach another device: no remote copies, remote signals or barrier semaphores. Data moves between devices by JAX's collectives and lax.ppermute only.
A program may use at most 128 MiB of HBM per device.

```python
import math
import jax
import jax.numpy as jnp
import numpy as np
from jax import lax

D = 768
HEADS = 12
HD = 64
L = 64
NT = 2
K = 32
CEN_DEV = 32
OWN_DEV = 2048
CENTRES = 2048
OWNED = 131072
OWNERS = 64
REQ_DEV = 2048
CAP = 32
N_NODES = 64


def shared_query(key):
    return jax.random.normal(jax.random.fold_in(key, 7001), (D, D), jnp.float32) / math.sqrt(D)


def draw_w_query(key, part):
    return jnp.clip(shared_query(key), -0.5, 0.5).astype(jnp.bfloat16)


def draw_w_key(key, part):
    fresh_noise = jax.random.normal(jax.random.fold_in(key, 7002), (D, D), jnp.float32) / math.sqrt(D)
    mixed = fresh_noise
    return jnp.clip(mixed, -0.5, 0.5).astype(jnp.bfloat16)


def draw_tokens(key, part):
    normal_draw = jax.random.normal(jax.random.fold_in(key, 7010), (CENTRES, L, D), jnp.float32)
    return jnp.clip(normal_draw, -32.0, 32.0).astype(jnp.bfloat16)


def with_ends(array, stream_key, smallest, top_value):
    longest = array.shape.index(max(array.shape))
    spots = []
    for shift in (0, 1):
        where = [jax.random.randint(jax.random.fold_in(stream_key, axis), (), 0, length) for axis, length in enumerate(array.shape)]
        where[longest] = (where[longest] + shift) % array.shape[longest]
        spots.append(tuple(where))
    return array.at[spots[0]].set(smallest).at[spots[1]].set(top_value)


def levels(own_key, extent, shards, smallest, largest):
    gain, own = 1.0, jax.random.fold_in(own_key, 6)
    for dim, parts in shards:
        steps = jnp.exp(jax.random.uniform(jax.random.fold_in(own, dim), (parts,), jnp.float32, smallest / len(shards), largest / len(shards)))
        gain = gain * jnp.repeat(steps, extent[dim] // parts).reshape([-1 if axis == dim else 1 for axis in range(len(extent))])
    return gain


def rank_table(number_of, skew):
    loads = [(1 << 20) // math.isqrt(rank ** skew) + 1 for rank in range(1, number_of + 1)]
    spread = 1 + sum(loads) // (1 << 30)
    return np.cumsum(np.array([max(1, weight // spread) for weight in loads]))


def skewed_ids(key, dims, count, slope):
    table = rank_table(count, slope)
    ticket = jax.random.randint(jax.random.fold_in(key, 1), dims, 0, int(table[count - 1]))
    standing = jnp.searchsorted(jnp.asarray(table, jnp.int32), ticket, side="right")
    return jax.random.permutation(jax.random.fold_in(key, 2), count)[standing].astype(jnp.int32)


def scatter_about(key, extent, spread, reach, split=(), kind=jnp.bfloat16):
    drawn = spread * jax.random.normal(key, extent, jnp.float32)
    if split:
        drawn = drawn * levels(key, extent, split, -0.22, 0.18)
    return jnp.clip(drawn, -reach, reach).astype(kind)


def setup_inputs(seed: int = 0) -> dict:
    key_of = jax.random.split(jax.random.key(seed), 10)
    tokens = draw_tokens(jax.random.fold_in(key_of[9], 71), 0)
    w_query = draw_w_query(jax.random.fold_in(key_of[9], 71), 0)
    w_key = draw_w_key(jax.random.fold_in(key_of[9], 71), 0)
    w_value = scatter_about(key_of[3], (D, D), D ** -0.5, 0.21875, ((0, 4),))
    grad_out = scatter_about(key_of[4], (CENTRES, HEADS, L * HD), 1.0, 6.0, ((0, 64), (1, 4)))
    owned_cls = scatter_about(key_of[5], (D, OWNED), 4.0, 24.0, ((0, 4), (1, 64)))
    send_rows = with_ends(skewed_ids(key_of[6], (OWNERS, OWNERS, CAP), OWN_DEV, 2), jax.random.fold_in(key_of[6], 3), 0, OWN_DEV - 1).astype(jnp.int32)
    neigh_slot = with_ends(jax.random.randint(key_of[7], (CENTRES, NT, K), 0, REQ_DEV), jax.random.fold_in(key_of[7], 1), 0, REQ_DEV - 1).astype(jnp.int32)
    neigh_count = with_ends(jax.random.randint(key_of[8], (CENTRES, NT), 1, K + 1), jax.random.fold_in(key_of[8], 1), 1, K).astype(jnp.int32)
    return dict(tokens=tokens, w_query=w_query, w_key=w_key, w_value=w_value, grad_out=grad_out, owned_cls=owned_cls, send_rows=send_rows, neigh_slot=neigh_slot, neigh_count=neigh_count)


def attend(text_tokens, virtual, query_weight, key_weight, value_weight, grad_text):
    centres = text_tokens.shape[0]
    key_input = jnp.concatenate([virtual, text_tokens], axis=1)
    flat_tokens = text_tokens.reshape(-1, D)
    flat_keys = key_input.reshape(-1, D)
    queries = jnp.dot(flat_tokens, query_weight, preferred_element_type=jnp.float32).astype(jnp.bfloat16).reshape(centres, L, HEADS, HD)
    keys = jnp.dot(flat_keys, key_weight, preferred_element_type=jnp.float32).astype(jnp.bfloat16).reshape(centres, NT + L, HEADS, HD)
    values = jnp.dot(flat_keys, value_weight, preferred_element_type=jnp.float32).astype(jnp.bfloat16).reshape(centres, NT + L, HEADS, HD)
    score_scale = 1.0 / math.sqrt(HD)
    scores = jnp.einsum('clhe,cmhe->chlm', queries.astype(jnp.float32), keys.astype(jnp.float32)) * score_scale
    attn_probs = jax.nn.softmax(scores, axis=-1)
    probs_low = attn_probs.astype(jnp.bfloat16)
    context = jnp.einsum('chlm,cmhe->clhe', probs_low.astype(jnp.float32), values.astype(jnp.float32)).astype(jnp.bfloat16)
    grad_heads = grad_text.reshape(centres, L, HEADS, HD).astype(jnp.float32)
    prob_grads = jnp.einsum('clhe,cmhe->chlm', grad_heads, values.astype(jnp.float32))
    value_grads = jnp.einsum('chlm,clhe->cmhe', probs_low.astype(jnp.float32), grad_heads).astype(jnp.bfloat16)
    score_grads = attn_probs * (prob_grads - lax.optimization_barrier(jnp.sum(prob_grads * attn_probs, axis=-1, keepdims=True))) * score_scale
    score_low = score_grads.astype(jnp.bfloat16).astype(jnp.float32)
    query_grads = jnp.einsum('chlm,cmhe->clhe', score_low, keys.astype(jnp.float32)).astype(jnp.bfloat16)
    key_grads = jnp.einsum('chlm,clhe->cmhe', score_low, queries.astype(jnp.float32)).astype(jnp.bfloat16)
    part_query = jnp.dot(flat_tokens.T, query_grads.reshape(-1, D), preferred_element_type=jnp.float32)
    part_key = jnp.dot(flat_keys.T, key_grads.reshape(-1, D), preferred_element_type=jnp.float32)
    part_value = jnp.dot(flat_keys.T, value_grads.reshape(-1, D), preferred_element_type=jnp.float32)
    virtual_key = key_grads[:, :NT].reshape(-1, D)
    virtual_value = value_grads[:, :NT].reshape(-1, D)
    virtual_grads = jnp.dot(virtual_key, key_weight.T, preferred_element_type=jnp.float32) + jnp.dot(virtual_value, value_weight.T, preferred_element_type=jnp.float32)
    return (context, part_query, part_key, part_value, virtual_grads.reshape(centres, NT, D))

def reference(tokens, w_query, w_key, w_value, grad_out, owned_cls, send_rows, neigh_slot, neigh_count):
    query_weight = w_query.T
    key_weight = w_key.T
    value_weight = w_value.T
    owned_blocks = owned_cls.T.reshape(N_NODES, OWN_DEV, D)
    token_blocks = tokens.reshape(N_NODES, CEN_DEV, L, D)
    grad_text = grad_out.reshape(CENTRES, HEADS, L, HD).transpose(0, 2, 1, 3).reshape(CENTRES, L, D)
    grad_blocks = grad_text.reshape(N_NODES, CEN_DEV, L, D)
    slot_blocks = neigh_slot.reshape(N_NODES, CEN_DEV, NT, K)
    count_blocks = neigh_count.reshape(N_NODES, CEN_DEV, NT)
    owner_ids = jnp.arange(N_NODES, dtype=jnp.int32)[:, None]
    positions = jnp.arange(K, dtype=jnp.int32)

    def per_device(totals, device_index):
        total_query, total_key, total_value, cls_total = totals
        rows_sent = send_rows[:, device_index, :]
        fetched = owned_blocks[owner_ids, rows_sent].reshape(REQ_DEV, D)
        slots = slot_blocks[device_index]
        counts = count_blocks[device_index]
        live_mask = (positions[None, None, :] < counts[:, :, None]).astype(jnp.float32)
        picked = fetched[slots].astype(jnp.float32)
        denominator = counts.astype(jnp.float32)
        virtual = (lax.optimization_barrier(jnp.sum(live_mask[..., None] * picked, axis=2)) / denominator[..., None]).astype(jnp.bfloat16)
        context, part_query, part_key, part_value, virtual_grads = attend(token_blocks[device_index], virtual, query_weight, key_weight, value_weight, grad_blocks[device_index])
        shared_grad = virtual_grads / denominator[..., None]
        slot_terms = (live_mask[..., None] * shared_grad[:, :, None, :]).reshape(-1, D)
        slot_grads = jax.ops.segment_sum(slot_terms, slots.reshape(-1), num_segments=REQ_DEV).reshape(N_NODES, CAP, D)
        cls_total = cls_total.at[owner_ids, rows_sent].add(slot_grads)
        return ((total_query + part_query, total_key + part_key, total_value + part_value, cls_total), context)
    zero_weight = jnp.zeros((D, D), jnp.float32)
    start_totals = (zero_weight, zero_weight, zero_weight, jnp.zeros((N_NODES, OWN_DEV, D), jnp.float32))
    totals, contexts = lax.scan(per_device, start_totals, jnp.arange(N_NODES, dtype=jnp.int32))
    grad_query, grad_key, grad_value, cls_total = totals
    context = contexts.reshape(CENTRES, L, HEADS, HD).transpose(0, 2, 1, 3).reshape(CENTRES, HEADS, L * HD)
    return (context, grad_query.T, grad_key.T, grad_value.T, cls_total.reshape(OWNED, D).T)
```

```python
import jax
import jax.numpy as jnp
from jax import lax
from jax.experimental import pallas as pl
from jax.experimental.pallas import tpu as pltpu
from jax.sharding import PartitionSpec as P

HD = 64
BF = jnp.bfloat16
F32 = jnp.float32
CHIPS = 32
CENTRES = 32
GROUP = 4
VMEM_LIMIT = 60 * 1024 * 1024

XZ_GROUPS = [[chip * 2 + core for chip in range(CHIPS)] for core in range(2)]
CORE_SWAP = [(dev, dev ^ 1) for dev in range(2 * CHIPS)]


def nt(a, b):
    return lax.dot_general(a, b, (((1,), (1,)), ((), ())), preferred_element_type=F32)


def nn(a, b):
    return lax.dot_general(a, b, (((1,), (0,)), ((), ())), preferred_element_type=F32)


def tn(a, b):
    return lax.dot_general(a, b, (((0,), (0,)), ((), ())), preferred_element_type=F32)


def core_swap(x):
    return lax.ppermute(x, "nodes", CORE_SWAP)


def chip_exchange(x):
    return lax.all_to_all(
        x, "nodes", split_axis=0, concat_axis=0, tiled=True, axis_index_groups=XZ_GROUPS
    )


def gather_kernel(index_ref, table_ref, out_ref):
    rows = table_ref.shape[1]
    row = lax.broadcasted_iota(jnp.int32, (rows, 256), 0)
    select = jnp.where(row == index_ref[0], 1.0, 0.0).astype(BF)
    picked = nn(table_ref[...], select)
    turned = picked.T.astype(BF)
    for chip in range(4):
        own = turned[32 * chip : 32 * chip + 32]
        other = turned[128 + 32 * chip : 160 + 32 * chip]
        out_ref[chip, 0:32, :] = own[:, 0:128]
        out_ref[chip, 32:64, :] = other[:, 0:128]
        out_ref[chip, 64:96, 0:64] = own[:, 128:192]
        out_ref[chip, 64:96, 64:128] = other[:, 128:192]


def gather_rows(index, table):
    rows = table.shape[1]
    return pl.pallas_call(
        gather_kernel,
        out_shape=jax.ShapeDtypeStruct((CHIPS, 96, 128), BF),
        grid=(8,),
        in_specs=[
            pl.BlockSpec((1, 1, 256), lambda i: (i, 0, 0)),
            pl.BlockSpec((192, rows), lambda i: (0, 0)),
        ],
        out_specs=pl.BlockSpec((4, 96, 128), lambda i: (i, 0, 0)),
        compiler_params=pltpu.CompilerParams(vmem_limit_bytes=VMEM_LIMIT),
        name="gather_rows",
    )(index, table)


def mixing_kernel(key_ref, out_ref):
    for block in range(8):
        slot = lax.broadcasted_iota(jnp.int32, (128, 128), 0) + 128 * block
        total = jnp.zeros((128, 128), F32)
        for k in range(32):
            total = total + jnp.where(slot == key_ref[k : k + 1, :], 1.0, 0.0)
        out_ref[128 * block : 128 * block + 128, :] = total.astype(BF)


def make_mixing(keys):
    return pl.pallas_call(
        mixing_kernel,
        out_shape=jax.ShapeDtypeStruct((1024, 128), BF),
        name="make_mixing",
    )(keys)


def virtual_kernel(rows_ref, mix_ref, own_ref, other_ref):
    mix = mix_ref[...]
    first = tn(mix, rows_ref[:, 0:32, :].reshape(1024, 128))
    second = tn(mix, rows_ref[:, 32:64, :].reshape(1024, 128))
    both = tn(mix, rows_ref[:, 64:96, :].reshape(1024, 128))
    own_ref[:, 0:128] = first[0:64]
    own_ref[:, 128:192] = both[0:64, 0:64]
    other_ref[:, 0:128] = second[64:128]
    other_ref[:, 128:192] = both[64:128, 64:128]


def mix_rows(rows, mix):
    part = jax.ShapeDtypeStruct((64, 192), F32)
    return pl.pallas_call(virtual_kernel, out_shape=(part, part), name="mix_rows")(rows, mix)


def attend_kernel(
    place_ref, tok_ref, grad_ref, virt_ref, wq_ref, wk_ref, wv_ref, wk4_ref, wv4_ref,
    ctx_ref, dw_ref, vg0_ref, vg1_ref, vg2_ref, vg3_ref,
    acc_ref, kvirt_ref, vvirt_ref, dkvirt_ref, dvvirt_ref,
):
    step = pl.program_id(0)
    width = 192

    @pl.when(step == 0)
    def _():
        acc_ref[...] = jnp.zeros_like(acc_ref)
        row = lax.broadcasted_iota(jnp.int32, (512, 64), 0)
        pair = lax.broadcasted_iota(jnp.int32, (512, 64), 1)
        spread = jnp.where((row // 16 == pair // 2) & (row % 16 == pair % 2), 1.0, 0.0).astype(BF)
        virt = virt_ref[...]
        kvirt_ref[...] = nn(spread, nt(virt, wk_ref[...]).astype(BF)).astype(BF)
        vvirt_ref[...] = nn(spread, nt(virt, wv_ref[...]).astype(BF)).astype(BF)

    tok = tok_ref[...]
    queries = nt(tok, wq_ref[...]).astype(BF)
    keys = nt(tok, wk_ref[...]).astype(BF)
    values = nt(tok, wv_ref[...]).astype(BF)
    head_row = lax.broadcasted_iota(jnp.int32, (width, width), 0) // HD
    head_col = lax.broadcasted_iota(jnp.int32, (width, width), 1) // HD
    blocks = jnp.where(head_row == head_col, 1.0, 0.0).astype(BF)
    valid = lax.broadcasted_iota(jnp.int32, (80, width), 0) < 66
    lane = lax.broadcasted_iota(jnp.int32, (HD, width), 1)

    def heads_of(full):
        return jnp.where(
            lane < 64, full[0:64], jnp.where(lane < 128, full[64:128], full[128:192])
        )

    dqs, dks, dvs = [], [], []
    for i in range(GROUP):
        at = pl.multiple_of((step * GROUP + i) * 16, 16)
        span = slice(64 * i, 64 * i + 64)
        key = jnp.concatenate([keys[span], kvirt_ref[pl.ds(at, 16), :]], axis=0)
        value = jnp.concatenate([values[span], vvirt_ref[pl.ds(at, 16), :]], axis=0)
        query = queries[span]
        grad = grad_ref[span, :]
        query_blocks = jnp.concatenate([query, query, query], axis=0) * blocks
        grad_blocks = jnp.concatenate([grad, grad, grad], axis=0) * blocks
        scores = jnp.where(valid, nt(key, query_blocks) * 0.125, -1e30)
        top = jnp.max(scores, axis=0, keepdims=True)
        powers = jnp.exp(scores - top)
        powers = jnp.where(valid, powers, 0.0)
        probs = powers * (1.0 / jnp.sum(powers, axis=0, keepdims=True))
        low = probs.astype(BF)
        prob_grads = nt(value, grad_blocks)
        inner = jnp.sum(prob_grads * probs, axis=0, keepdims=True)
        score_low = (probs * (prob_grads - inner) * 0.125).astype(BF)
        ctx_ref[span, :] = heads_of(tn(low, value)).astype(BF)
        dq = heads_of(tn(score_low, key)).astype(BF)
        dv = nn(low, grad_blocks).astype(BF)
        dk = nn(score_low, query_blocks).astype(BF)
        dkvirt_ref[pl.ds(at, 16), :] = dk[64:80]
        dvvirt_ref[pl.ds(at, 16), :] = dv[64:80]
        dqs.append(dq)
        dks.append(dk[0:64])
        dvs.append(dv[0:64])
    acc_ref[0:192, :] += tn(jnp.concatenate(dqs, axis=0), tok)
    acc_ref[192:384, :] += tn(jnp.concatenate(dks, axis=0), tok)
    acc_ref[384:576, :] += tn(jnp.concatenate(dvs, axis=0), tok)

    @pl.when(step == pl.num_programs(0) - 1)
    def _():
        pair = lax.broadcasted_iota(jnp.int32, (64, 512), 0)
        row = lax.broadcasted_iota(jnp.int32, (64, 512), 1)
        collect = jnp.where((row // 16 == pair // 2) & (row % 16 == pair % 2), 1.0, 0.0).astype(BF)
        dk = nn(collect, dkvirt_ref[...]).astype(BF)
        dv = nn(collect, dvvirt_ref[...]).astype(BF)
        virt = virt_ref[...]
        acc_ref[192:384, :] += tn(dk, virt)
        acc_ref[384:576, :] += tn(dv, virt)
        own = place_ref[0]
        for d, ref in enumerate((vg0_ref, vg1_ref, vg2_ref, vg3_ref)):
            at = (own + d) % 4
            ref[...] = (nn(dk, wk4_ref[at]) + nn(dv, wv4_ref[at])).astype(ref.dtype)
        for core in range(2):
            @pl.when(place_ref[1] == core)
            def _():
                for t in range(3):
                    keep = 3 * core + t
                    give = 3 * (1 - core) + t
                    dw_ref[0, t] = acc_ref[:, 128 * keep : 128 * keep + 128]
                    dw_ref[1, t] = acc_ref[:, 128 * give : 128 * give + 128]


def attend(place, tokens, grads, virtual, wq, wk, wv, wk4, wv4):
    rows = 64 * GROUP
    steps = CENTRES // GROUP
    fixed2 = lambda i: (0, 0)
    fixed3 = lambda i: (0, 0, 0)
    out_shape = (
        jax.ShapeDtypeStruct((2048, 192), BF),
        jax.ShapeDtypeStruct((2, 3, 576, 128), F32),
        jax.ShapeDtypeStruct((64, 192), F32),
        jax.ShapeDtypeStruct((64, 192), BF),
        jax.ShapeDtypeStruct((64, 192), BF),
        jax.ShapeDtypeStruct((64, 192), BF),
    )
    small = pl.BlockSpec((64, 192), fixed2)
    weight = pl.BlockSpec((192, 768), fixed2)
    return pl.pallas_call(
        attend_kernel,
        out_shape=out_shape,
        grid=(steps,),
        in_specs=[
            pl.BlockSpec(memory_space=pltpu.SMEM),
            pl.BlockSpec((rows, 768), lambda i: (i, 0)),
            pl.BlockSpec((rows, 192), lambda i: (i, 0)),
            pl.BlockSpec((64, 768), fixed2),
            weight, weight, weight,
            pl.BlockSpec((4, 192, 192), fixed3),
            pl.BlockSpec((4, 192, 192), fixed3),
        ],
        out_specs=(
            pl.BlockSpec((rows, 192), lambda i: (i, 0)),
            pl.BlockSpec((2, 3, 576, 128), lambda i: (0, 0, 0, 0)),
            small, small, small, small,
        ),
        scratch_shapes=[
            pltpu.VMEM((576, 768), F32),
            pltpu.VMEM((512, 192), BF),
            pltpu.VMEM((512, 192), BF),
            pltpu.VMEM((512, 192), BF),
            pltpu.VMEM((512, 192), BF),
        ],
        compiler_params=pltpu.CompilerParams(vmem_limit_bytes=VMEM_LIMIT),
        name="attend",
    )(place, tokens, grads, virtual, wq, wk, wv, wk4, wv4)


def spread_kernel(own_ref, other_ref, mix_ref, weights_ref, out_ref):
    mix = mix_ref[...]
    zeros = jnp.zeros((64, 192), BF)

    def split(x):
        high = x.astype(BF)
        return high, (x - high.astype(F32)).astype(BF)

    own_high, own_low = split(own_ref[...])
    other_high, other_low = split(other_ref[...])
    stack = lambda a, b: jnp.concatenate([a, b], axis=0)
    own = nn(mix, stack(own_high, zeros)) + nn(mix, stack(own_low, zeros))
    other = nn(mix, stack(zeros, other_high)) + nn(mix, stack(zeros, other_low))
    own = own.astype(BF)
    other = other.astype(BF)
    out_ref[:, 0:32, :] = own[:, 0:128].reshape(CHIPS, 32, 128)
    out_ref[:, 32:64, :] = other[:, 0:128].reshape(CHIPS, 32, 128)
    out_ref[:, 64:96, 0:64] = own[:, 128:192].reshape(CHIPS, 32, 64)
    out_ref[:, 64:96, 64:128] = other[:, 128:192].reshape(CHIPS, 32, 64)
    total = weights_ref[0].astype(F32)
    for chip in range(1, CHIPS):
        total = total + weights_ref[chip].astype(F32)
    total = total.astype(BF)
    for chip in range(CHIPS):
        out_ref[chip, 96:160, :] = total


def spread(own, other, mix, weights):
    return pl.pallas_call(
        spread_kernel,
        out_shape=jax.ShapeDtypeStruct((CHIPS, 160, 128), BF),
        name="spread",
    )(own, other, mix, weights)


def scatter_kernel(index_ref, rows_ref, out_ref, turned_ref):
    step = pl.program_id(0)

    @pl.when(step == 0)
    def _():
        for g in range(8):
            chips = slice(4 * g, 4 * g + 4)
            first = rows_ref[chips, 0:32, :].reshape(128, 128).astype(F32).T.astype(BF)
            second = rows_ref[chips, 32:64, :].reshape(128, 128).astype(F32).T.astype(BF)
            both = rows_ref[chips, 64:96, :].reshape(128, 128).astype(F32).T.astype(BF)
            lanes = slice(256 * g, 256 * g + 128)
            more = slice(256 * g + 128, 256 * g + 256)
            turned_ref[0:128, lanes] = first
            turned_ref[128:192, lanes] = both[0:64]
            turned_ref[0:128, more] = second
            turned_ref[128:192, more] = both[64:128]

    row = lax.broadcasted_iota(jnp.int32, (256, 2048), 0) + 256 * step
    select = jnp.where(row == index_ref[...], 1.0, 0.0).astype(BF)
    out_ref[...] = nt(turned_ref[...], select)


def scatter_rows(index, rows):
    return pl.pallas_call(
        scatter_kernel,
        out_shape=jax.ShapeDtypeStruct((192, 2048), F32),
        grid=(8,),
        in_specs=[
            pl.BlockSpec((1, 2048), lambda i: (0, 0)),
            pl.BlockSpec((CHIPS, 96, 128), lambda i: (0, 0, 0)),
        ],
        out_specs=pl.BlockSpec((192, 256), lambda i: (0, i)),
        scratch_shapes=[pltpu.VMEM((192, 2048), BF)],
        compiler_params=pltpu.CompilerParams(vmem_limit_bytes=VMEM_LIMIT),
        name="scatter_rows",
    )(index, rows)


def body(tokens, w_query, w_key, w_value, grad_out, owned_cls, send_rows, neigh_slot, neigh_count):
    core = lax.axis_index("nodes") % 2
    own_mp = lax.axis_index("mp")
    place = jnp.stack([own_mp, core]).astype(jnp.int32)

    asked = send_rows.reshape(8, 4, 2, 32)
    asked = jnp.where(core == 0, asked, asked[:, :, ::-1])
    index = asked.transpose(0, 2, 1, 3).reshape(8, 1, 256)
    sent = gather_rows(index, owned_cls)

    slots = neigh_slot.reshape(64, 32)
    counts = neigh_count.reshape(64, 1)
    position = lax.broadcasted_iota(jnp.int32, (64, 32), 1)
    slots = jnp.where(position < counts, slots, -1)
    all_slots = jnp.concatenate([slots, core_swap(slots)], axis=0)
    here = (all_slots >= 0) & (((all_slots >> 5) & 1) == core)
    keys = jnp.where(here, (all_slots >> 6) * 32 + (all_slots & 31), -1).T
    mix = make_mixing(keys)

    heads = grad_out.reshape(32, 3, 64, 64).transpose(0, 2, 1, 3).reshape(2048, 192)
    wk4 = w_key.reshape(192, 4, 192).transpose(1, 0, 2)
    wv4 = w_value.reshape(192, 4, 192).transpose(1, 0, 2)

    fetched = chip_exchange(sent)
    own_part, other_part = mix_rows(fetched, mix)
    divisor = counts.astype(F32)
    local = ((own_part + core_swap(other_part)) / divisor).astype(BF)
    virtual = lax.all_gather(local, "mp", axis=1, tiled=True)

    ctx, dw, vg0, vg1, vg2, vg3 = attend(
        place, tokens.reshape(2048, 768), heads, virtual, w_query, w_key, w_value, wk4, wv4
    )
    context = ctx.reshape(32, 64, 3, 64).transpose(0, 2, 1, 3).reshape(32, 3, 4096)

    around = lambda x, d: lax.ppermute(x, "mp", [(i, (i + d) % 4) for i in range(4)])
    moved = [around(vg, d + 1) for d, vg in enumerate((vg1, vg2, vg3))]
    half = dw[0] + core_swap(dw[1])
    half = half.astype(BF).reshape(1728, 128)
    padded = jnp.pad(half, ((0, 2048 - 1728), (0, 0))).reshape(CHIPS, 64, 128)
    pieces = chip_exchange(padded)

    shared = (vg0 + moved[0].astype(F32) + moved[1].astype(F32) + moved[2].astype(F32)) / divisor
    other_shared = core_swap(shared)
    outgoing = spread(shared, other_shared, mix, pieces)
    arrived = chip_exchange(outgoing)

    mine = arrived[:, 96:160].reshape(2048, 128)[:1728]
    theirs = core_swap(mine)
    grad_cls = scatter_rows(index.reshape(1, 2048), arrived)
    first = jnp.where(core == 0, mine, theirs).reshape(3, 576, 128)
    second = jnp.where(core == 0, theirs, mine).reshape(3, 576, 128)
    grads = jnp.concatenate([first, second], axis=0).transpose(1, 0, 2).reshape(576, 768).astype(F32)
    return (context, grads[0:192], grads[192:384], grads[384:576], grad_cls)


def solution(mesh):
    in_specs = (
        P("nodes", None, None),
        P("mp", None),
        P("mp", None),
        P("mp", None),
        P("nodes", "mp", None),
        P("mp", "nodes"),
        P("nodes", None, None),
        P("nodes", None, None),
        P("nodes", None),
    )
    out_specs = (
        P("nodes", "mp", None),
        P("mp", None),
        P("mp", None),
        P("mp", None),
        P("mp", "nodes"),
    )
    return jax.shard_map(body, mesh=mesh, in_specs=in_specs, out_specs=out_specs, check_vma=False)
```

```python
import jax
import jax.numpy as jnp
from jax import lax
from jax.experimental import pallas as pl
from jax.experimental.pallas import tpu as pltpu
from jax.sharding import PartitionSpec as P


HD = 64
BF = jnp.bfloat16
F32 = jnp.float32
CHIPS = 32
CENTRES = 32
GROUP = 4
VMEM_LIMIT = 60 * 1024 * 1024

XZ_GROUPS = [[chip * 2 + core for chip in range(CHIPS)] for core in range(2)]
CORE_SWAP = [(dev, dev ^ 1) for dev in range(2 * CHIPS)]


def nt(a, b):
    return lax.dot_general(a, b, (((1,), (1,)), ((), ())), preferred_element_type=F32)


def nn(a, b):
    return lax.dot_general(a, b, (((1,), (0,)), ((), ())), preferred_element_type=F32)


def tn(a, b):
    return lax.dot_general(a, b, (((0,), (0,)), ((), ())), preferred_element_type=F32)


def core_swap(x):
    return lax.ppermute(x, "nodes", CORE_SWAP)


def along(x, dx, dz):
    pairs = []
    for dev in range(2 * CHIPS):
        at_x, at_z, core = dev // 16, dev // 2 % 8, dev % 2
        pairs.append((dev, ((at_x + dx) % 4 * 8 + (at_z + dz) % 8) * 2 + core))
    return lax.ppermute(x, "nodes", pairs)


def chip_exchange(x):
    return lax.all_to_all(
        x, "nodes", split_axis=0, concat_axis=0, tiled=True, axis_index_groups=XZ_GROUPS
    )


def gather_kernel(index_ref, table_ref, out_ref):
    rows = table_ref.shape[1]
    row = lax.broadcasted_iota(jnp.int32, (rows, 256), 0)
    select = jnp.where(row == index_ref[0], 1.0, 0.0).astype(BF)
    picked = nn(table_ref[...], select)
    turned = picked.T.astype(BF)
    for chip in range(4):
        own = turned[32 * chip : 32 * chip + 32]
        other = turned[128 + 32 * chip : 160 + 32 * chip]
        out_ref[chip, 0:32, :] = own[:, 0:128]
        out_ref[chip, 32:64, :] = other[:, 0:128]
        out_ref[chip, 64:96, 0:64] = own[:, 128:192]
        out_ref[chip, 64:96, 64:128] = other[:, 128:192]


def gather_rows(index, table):
    rows = table.shape[1]
    return pl.pallas_call(
        gather_kernel,
        out_shape=jax.ShapeDtypeStruct((CHIPS, 96, 128), BF),
        grid=(8,),
        in_specs=[
            pl.BlockSpec((1, 1, 256), lambda i: (i, 0, 0)),
            pl.BlockSpec((192, rows), lambda i: (0, 0)),
        ],
        out_specs=pl.BlockSpec((4, 96, 128), lambda i: (i, 0, 0)),
        compiler_params=pltpu.CompilerParams(vmem_limit_bytes=VMEM_LIMIT),
        name="gather_rows",
    )(index, table)


def mixing_kernel(key_ref, out_ref):
    for block in range(8):
        slot = lax.broadcasted_iota(jnp.int32, (128, 128), 0) + 128 * block
        total = jnp.zeros((128, 128), F32)
        for k in range(32):
            total = total + jnp.where(slot == key_ref[k : k + 1, :], 1.0, 0.0)
        out_ref[128 * block : 128 * block + 128, :] = total.astype(BF)


def make_mixing(keys):
    return pl.pallas_call(
        mixing_kernel,
        out_shape=jax.ShapeDtypeStruct((1024, 128), BF),
        name="make_mixing",
    )(keys)


def virtual_kernel(rows_ref, mix_ref, *refs):
    own_ref, other_ref = refs[-2:]
    mix = mix_ref[...]
    first = tn(mix, rows_ref[:, 0:32, :].reshape(1024, 128))
    second = tn(mix, rows_ref[:, 32:64, :].reshape(1024, 128))
    both = tn(mix, rows_ref[:, 64:96, :].reshape(1024, 128))
    own_ref[:, 0:128] = first[0:64]
    own_ref[:, 128:192] = both[0:64, 0:64]
    other_ref[:, 0:128] = second[64:128]
    other_ref[:, 128:192] = both[64:128, 64:128]


def mix_rows(rows, mix, *after):
    part = jax.ShapeDtypeStruct((64, 192), F32)
    whole = pl.BlockSpec(memory_space=pltpu.VMEM)
    return pl.pallas_call(
        virtual_kernel,
        out_shape=(part, part),
        in_specs=[whole, whole] + [pl.BlockSpec(memory_space=pl.ANY)] * len(after),
        name="mix_rows",
    )(rows, mix, *after)


def project_kernel(tok_ref, wq_ref, wk_ref, wv_ref, q_ref, k_ref, v_ref):
    tok = tok_ref[...]
    q_ref[...] = nt(tok, wq_ref[...]).astype(BF)
    k_ref[...] = nt(tok, wk_ref[...]).astype(BF)
    v_ref[...] = nt(tok, wv_ref[...]).astype(BF)


def project(tokens, wq, wk, wv):
    out = jax.ShapeDtypeStruct((2048, 192), BF)
    weight = pl.BlockSpec((192, 768), lambda i: (0, 0))
    block = pl.BlockSpec((512, 192), lambda i: (i, 0))
    return pl.pallas_call(
        project_kernel,
        out_shape=(out, out, out),
        grid=(4,),
        in_specs=[pl.BlockSpec((512, 768), lambda i: (i, 0)), weight, weight, weight],
        out_specs=(block, block, block),
        compiler_params=pltpu.CompilerParams(vmem_limit_bytes=VMEM_LIMIT),
        name="project",
    )(tokens, wq, wk, wv)


def attend_kernel(
    place_ref, tok_ref, q_ref, k_ref, v_ref, grad_ref, virt_ref, wk_ref, wv_ref, wk4_ref, wv4_ref,
    ctx_ref, keep_ref, give_ref, vg0_ref, vg1_ref, vg2_ref, vg3_ref,
    acc_ref, kvirt_ref, vvirt_ref, dkvirt_ref, dvvirt_ref,
):
    step = pl.program_id(0)
    width = 192

    @pl.when(step == 0)
    def _():
        acc_ref[...] = jnp.zeros_like(acc_ref)
        row = lax.broadcasted_iota(jnp.int32, (512, 64), 0)
        pair = lax.broadcasted_iota(jnp.int32, (512, 64), 1)
        spread = jnp.where((row // 16 == pair // 2) & (row % 16 == pair % 2), 1.0, 0.0).astype(BF)
        virt = virt_ref[...]
        kvirt_ref[...] = nn(spread, nt(virt, wk_ref[...]).astype(BF)).astype(BF)
        vvirt_ref[...] = nn(spread, nt(virt, wv_ref[...]).astype(BF)).astype(BF)

    tok = tok_ref[...]
    head_row = lax.broadcasted_iota(jnp.int32, (width, width), 0) // HD
    head_col = lax.broadcasted_iota(jnp.int32, (width, width), 1) // HD
    blocks = jnp.where(head_row == head_col, 1.0, 0.0).astype(BF)
    valid = lax.broadcasted_iota(jnp.int32, (80, width), 0) < 66
    lane = lax.broadcasted_iota(jnp.int32, (HD, width), 1)

    def heads_of(full):
        return jnp.where(
            lane < 64, full[0:64], jnp.where(lane < 128, full[64:128], full[128:192])
        )

    dqs, dks, dvs = [], [], []
    for i in range(GROUP):
        at = pl.multiple_of((step * GROUP + i) * 16, 16)
        span = slice(64 * i, 64 * i + 64)
        key = jnp.concatenate([k_ref[span, :], kvirt_ref[pl.ds(at, 16), :]], axis=0)
        value = jnp.concatenate([v_ref[span, :], vvirt_ref[pl.ds(at, 16), :]], axis=0)
        query = q_ref[span, :]
        grad = grad_ref[span, :]
        query_blocks = jnp.concatenate([query, query, query], axis=0) * blocks
        grad_blocks = jnp.concatenate([grad, grad, grad], axis=0) * blocks
        scores = jnp.where(valid, nt(key, query_blocks) * 0.125, -1e30)
        top = jnp.max(scores, axis=0, keepdims=True)
        powers = jnp.exp(scores - top)
        powers = jnp.where(valid, powers, 0.0)
        probs = powers * (1.0 / jnp.sum(powers, axis=0, keepdims=True))
        low = probs.astype(BF)
        prob_grads = nt(value, grad_blocks)
        inner = jnp.sum(prob_grads * probs, axis=0, keepdims=True)
        score_low = (probs * (prob_grads - inner) * 0.125).astype(BF)
        ctx_ref[span, :] = heads_of(tn(low, value)).astype(BF)
        dq = heads_of(tn(score_low, key)).astype(BF)
        dv = nn(low, grad_blocks).astype(BF)
        dk = nn(score_low, query_blocks).astype(BF)
        dkvirt_ref[pl.ds(at, 16), :] = dk[64:80]
        dvvirt_ref[pl.ds(at, 16), :] = dv[64:80]
        dqs.append(dq)
        dks.append(dk[0:64])
        dvs.append(dv[0:64])
    acc_ref[0:192, :] += tn(jnp.concatenate(dqs, axis=0), tok)
    acc_ref[192:384, :] += tn(jnp.concatenate(dks, axis=0), tok)
    acc_ref[384:576, :] += tn(jnp.concatenate(dvs, axis=0), tok)

    @pl.when(step == pl.num_programs(0) - 1)
    def _():
        pair = lax.broadcasted_iota(jnp.int32, (64, 512), 0)
        row = lax.broadcasted_iota(jnp.int32, (64, 512), 1)
        collect = jnp.where((row // 16 == pair // 2) & (row % 16 == pair % 2), 1.0, 0.0).astype(BF)
        dk = nn(collect, dkvirt_ref[...]).astype(BF)
        dv = nn(collect, dvvirt_ref[...]).astype(BF)
        virt = virt_ref[...]
        acc_ref[192:384, :] += tn(dk, virt)
        acc_ref[384:576, :] += tn(dv, virt)
        own = place_ref[0]
        for d, ref in enumerate((vg0_ref, vg1_ref, vg2_ref, vg3_ref)):
            at = (own + d) % 4
            ref[...] = (nn(dk, wk4_ref[at]) + nn(dv, wv4_ref[at])).astype(ref.dtype)
        for core in range(2):
            @pl.when(place_ref[1] == core)
            def _():
                for t in range(3):
                    keep = 3 * core + t
                    give = 3 * (1 - core) + t
                    keep_ref[t] = acc_ref[:, 128 * keep : 128 * keep + 128]
                    give_ref[t] = acc_ref[:, 128 * give : 128 * give + 128]


def attend(place, tokens, q, k, v, grads, virtual, wk, wv, wk4, wv4):
    rows = 64 * GROUP
    steps = CENTRES // GROUP
    fixed2 = lambda i: (0, 0)
    fixed3 = lambda i: (0, 0, 0)
    out_shape = (
        jax.ShapeDtypeStruct((2048, 192), BF),
        jax.ShapeDtypeStruct((3, 576, 128), F32),
        jax.ShapeDtypeStruct((3, 576, 128), F32),
        jax.ShapeDtypeStruct((64, 192), F32),
        jax.ShapeDtypeStruct((64, 192), BF),
        jax.ShapeDtypeStruct((64, 192), BF),
        jax.ShapeDtypeStruct((64, 192), BF),
    )
    small = pl.BlockSpec((64, 192), fixed2)
    weight = pl.BlockSpec((192, 768), fixed2)
    head = pl.BlockSpec((rows, 192), lambda i: (i, 0))
    half = pl.BlockSpec((3, 576, 128), fixed3)
    return pl.pallas_call(
        attend_kernel,
        out_shape=out_shape,
        grid=(steps,),
        in_specs=[
            pl.BlockSpec(memory_space=pltpu.SMEM),
            pl.BlockSpec((rows, 768), lambda i: (i, 0)),
            head, head, head, head,
            pl.BlockSpec((64, 768), fixed2),
            weight, weight,
            pl.BlockSpec((4, 192, 192), fixed3),
            pl.BlockSpec((4, 192, 192), fixed3),
        ],
        out_specs=(
            head, half, half,
            small, small, small, small,
        ),
        scratch_shapes=[
            pltpu.VMEM((576, 768), F32),
            pltpu.VMEM((512, 192), BF),
            pltpu.VMEM((512, 192), BF),
            pltpu.VMEM((512, 192), BF),
            pltpu.VMEM((512, 192), BF),
        ],
        compiler_params=pltpu.CompilerParams(vmem_limit_bytes=VMEM_LIMIT),
        name="attend",
    )(place, tokens, q, k, v, grads, virtual, wk, wv, wk4, wv4)


def spread_kernel(own_ref, other_ref, mix_ref, pieces_ref, *refs):
    out_ref, total_ref = refs[-2:]
    mix = mix_ref[...]
    zeros = jnp.zeros((64, 192), BF)

    def split(x):
        high = x.astype(BF)
        return high, (x - high.astype(F32)).astype(BF)

    own_high, own_low = split(own_ref[...])
    other_high, other_low = split(other_ref[...])
    stack = lambda a, b: jnp.concatenate([a, b], axis=0)
    own = nn(mix, stack(own_high, zeros)) + nn(mix, stack(own_low, zeros))
    other = nn(mix, stack(zeros, other_high)) + nn(mix, stack(zeros, other_low))
    own = own.astype(BF)
    other = other.astype(BF)
    out_ref[:, 0:32, :] = own[:, 0:128].reshape(CHIPS, 32, 128)
    out_ref[:, 32:64, :] = other[:, 0:128].reshape(CHIPS, 32, 128)
    out_ref[:, 64:96, 0:64] = own[:, 128:192].reshape(CHIPS, 32, 64)
    out_ref[:, 64:96, 64:128] = other[:, 128:192].reshape(CHIPS, 32, 64)
    total = pieces_ref[0].astype(F32)
    for chip in range(1, CHIPS):
        total = total + pieces_ref[chip].astype(F32)
    total_ref[...] = total.astype(BF)


def spread(own, other, mix, pieces, *after):
    whole = pl.BlockSpec(memory_space=pltpu.VMEM)
    return pl.pallas_call(
        spread_kernel,
        out_shape=(
            jax.ShapeDtypeStruct((CHIPS, 96, 128), BF),
            jax.ShapeDtypeStruct((64, 128), BF),
        ),
        in_specs=[whole] * 4 + [pl.BlockSpec(memory_space=pl.ANY)] * len(after),
        name="spread",
    )(own, other, mix, pieces, *after)


def assemble_kernel(place_ref, mine_ref, theirs_ref, after_ref, *out_refs):
    for piece in range(27):
        dx = (place_ref[2] - piece // 8 + 4) % 4
        dz = (place_ref[3] - piece % 8 + 8) % 8
        out_ref = out_refs[(piece % 9) // 3]
        rows = slice(64 * (piece % 3), 64 * (piece % 3) + 64)
        mine = mine_ref[dx, dz].astype(F32)
        theirs = theirs_ref[dx, dz].astype(F32)
        low = place_ref[1] == 0
        tile = 128 * (piece // 9)
        out_ref[rows, tile : tile + 128] = jnp.where(low, mine, theirs)
        out_ref[rows, 384 + tile : 512 + tile] = jnp.where(low, theirs, mine)


def assemble(place, mine, theirs, after):
    out = jax.ShapeDtypeStruct((192, 768), F32)
    whole = pl.BlockSpec(memory_space=pltpu.VMEM)
    return pl.pallas_call(
        assemble_kernel,
        out_shape=(out, out, out),
        in_specs=[
            pl.BlockSpec(memory_space=pltpu.SMEM), whole, whole, pl.BlockSpec(memory_space=pl.ANY)
        ],
        name="assemble",
    )(place, mine, theirs, after)


def scatter_kernel(index_ref, rows_ref, after_ref, out_ref, turned_ref):
    step = pl.program_id(0)

    @pl.when(step == 0)
    def _():
        for g in range(8):
            chips = slice(4 * g, 4 * g + 4)
            first = rows_ref[chips, 0:32, :].reshape(128, 128).astype(F32).T.astype(BF)
            second = rows_ref[chips, 32:64, :].reshape(128, 128).astype(F32).T.astype(BF)
            both = rows_ref[chips, 64:96, :].reshape(128, 128).astype(F32).T.astype(BF)
            lanes = slice(256 * g, 256 * g + 128)
            more = slice(256 * g + 128, 256 * g + 256)
            turned_ref[0:128, lanes] = first
            turned_ref[128:192, lanes] = both[0:64]
            turned_ref[0:128, more] = second
            turned_ref[128:192, more] = both[64:128]

    row = lax.broadcasted_iota(jnp.int32, (256, 2048), 0) + 256 * step
    select = jnp.where(row == index_ref[...], 1.0, 0.0).astype(BF)
    out_ref[...] = nt(turned_ref[...], select)


def scatter_rows(index, rows, after):
    return pl.pallas_call(
        scatter_kernel,
        out_shape=jax.ShapeDtypeStruct((192, 2048), F32),
        grid=(8,),
        in_specs=[
            pl.BlockSpec((1, 2048), lambda i: (0, 0)),
            pl.BlockSpec((CHIPS, 96, 128), lambda i: (0, 0, 0)),
            pl.BlockSpec(memory_space=pl.ANY),
        ],
        out_specs=pl.BlockSpec((192, 256), lambda i: (0, i)),
        scratch_shapes=[pltpu.VMEM((192, 2048), BF)],
        compiler_params=pltpu.CompilerParams(vmem_limit_bytes=VMEM_LIMIT),
        name="scatter_rows",
    )(index, rows, after)


def layer(tokens, w_query, w_key, w_value, grad_out, owned_cls, send_rows, neigh_slot, neigh_count):
    node = lax.axis_index("nodes")
    core = node % 2
    place = jnp.stack([lax.axis_index("mp"), core, node // 16, node // 2 % 8]).astype(jnp.int32)

    asked = send_rows.reshape(8, 4, 2, 32)
    asked = jnp.where(core == 0, asked, asked[:, :, ::-1])
    index = asked.transpose(0, 2, 1, 3).reshape(8, 1, 256)
    sent = gather_rows(index, owned_cls)

    slots = neigh_slot.reshape(64, 32)
    counts = neigh_count.reshape(64, 1)
    position = lax.broadcasted_iota(jnp.int32, (64, 32), 1)
    slots = jnp.where(position < counts, slots, -1)
    all_slots = jnp.concatenate([slots, core_swap(slots)], axis=0)
    here = (all_slots >= 0) & (((all_slots >> 5) & 1) == core)
    keys = jnp.where(here, (all_slots >> 6) * 32 + (all_slots & 31), -1).T
    mix = make_mixing(keys)

    heads = grad_out.reshape(32, 3, 64, 64).transpose(0, 2, 1, 3).reshape(2048, 192)
    wk4 = w_key.reshape(192, 4, 192).transpose(1, 0, 2)
    wv4 = w_value.reshape(192, 4, 192).transpose(1, 0, 2)

    flat = tokens.reshape(2048, 768)
    q, k, v = project(flat, w_query, w_key, w_value)

    fetched = chip_exchange(sent)
    own_part, other_part = mix_rows(fetched, mix, q, k, v, heads, wk4, wv4)
    divisor = counts.astype(F32)
    local = ((own_part + core_swap(other_part)) / divisor).astype(BF)
    virtual = lax.all_gather(local, "mp", axis=1, tiled=True)

    ctx, keep, give, vg0, vg1, vg2, vg3 = attend(
        place, flat, q, k, v, heads, virtual, w_key, w_value, wk4, wv4
    )
    context = ctx.reshape(32, 64, 3, 64).transpose(0, 2, 1, 3).reshape(32, 3, 4096)

    around = lambda x, d: lax.ppermute(x, "mp", [(i, (i + d) % 4) for i in range(4)])
    moved = [around(vg, d + 1) for d, vg in enumerate((vg1, vg2, vg3))]
    half = (keep + core_swap(give)).astype(BF).reshape(27, 64, 128)
    pieces = chip_exchange(jnp.pad(half, ((0, CHIPS - 27), (0, 0), (0, 0))))

    shared = (vg0 + moved[0].astype(F32) + moved[1].astype(F32) + moved[2].astype(F32)) / divisor
    outgoing, total = spread(
        shared, core_swap(shared), mix, pieces, context.transpose(1, 0, 2)
    )
    arrived = chip_exchange(outgoing)
    row = jnp.stack([total] + [along(total, 0, d) for d in range(1, 8)])
    mine = jnp.stack([row] + [along(row, d, 0) for d in range(1, 4)])
    theirs = core_swap(mine)
    grad_cls = scatter_rows(index.reshape(1, 2048), arrived, mine)
    grad_query, grad_key, grad_value = assemble(place, mine, theirs, grad_cls)
    return (context, grad_query, grad_key, grad_value, grad_cls)


def solution(mesh):
    in_specs = (
        P("nodes", None, None),
        P("mp", None),
        P("mp", None),
        P("mp", None),
        P("nodes", "mp", None),
        P("mp", "nodes"),
        P("nodes", None, None),
        P("nodes", None, None),
        P("nodes", None),
    )
    out_specs = (
        P("nodes", "mp", None),
        P("mp", None),
        P("mp", None),
        P("mp", None),
        P("mp", "nodes"),
    )
    return jax.shard_map(layer, mesh=mesh, in_specs=in_specs, out_specs=out_specs, check_vma=False)
```

```python
import jax
import jax.numpy as jnp
from jax import lax
from jax.experimental import pallas as pl
from jax.experimental.pallas import tpu as pltpu
from jax.sharding import PartitionSpec as P


HD = 64
BF = jnp.bfloat16
F32 = jnp.float32
CHIPS = 32
CENTRES = 32
GROUP = 8
VMEM_LIMIT = 60 * 1024 * 1024

XZ_GROUPS = [[chip * 2 + core for chip in range(CHIPS)] for core in range(2)]
CORE_SWAP = [(dev, dev ^ 1) for dev in range(2 * CHIPS)]


def nt(a, b):
    return lax.dot_general(a, b, (((1,), (1,)), ((), ())), preferred_element_type=F32)


def nn(a, b):
    return lax.dot_general(a, b, (((1,), (0,)), ((), ())), preferred_element_type=F32)


def tn(a, b):
    return lax.dot_general(a, b, (((0,), (0,)), ((), ())), preferred_element_type=F32)


def core_swap(x):
    return lax.ppermute(x, "nodes", CORE_SWAP)


def along(x, dx, dz):
    pairs = []
    for dev in range(2 * CHIPS):
        at_x, at_z, core = dev // 16, dev // 2 % 8, dev % 2
        pairs.append((dev, ((at_x + dx) % 4 * 8 + (at_z + dz) % 8) * 2 + core))
    return lax.ppermute(x, "nodes", pairs)


def chip_exchange(x):
    return lax.all_to_all(
        x, "nodes", split_axis=0, concat_axis=0, tiled=True, axis_index_groups=XZ_GROUPS
    )


def gather_kernel(index_ref, table_ref, out_ref):
    rows = table_ref.shape[1]
    row = lax.broadcasted_iota(jnp.int32, (rows, 256), 0)
    select = jnp.where(row == index_ref[0], 1.0, 0.0).astype(BF)
    picked = nn(table_ref[...], select)
    turned = picked.T.astype(BF)
    for chip in range(4):
        own = turned[32 * chip : 32 * chip + 32]
        other = turned[128 + 32 * chip : 160 + 32 * chip]
        out_ref[chip, 0:32, :] = own[:, 0:128]
        out_ref[chip, 32:64, :] = other[:, 0:128]
        out_ref[chip, 64:96, 0:64] = own[:, 128:192]
        out_ref[chip, 64:96, 64:128] = other[:, 128:192]


def gather_rows(index, table):
    rows = table.shape[1]
    return pl.pallas_call(
        gather_kernel,
        out_shape=jax.ShapeDtypeStruct((CHIPS, 96, 128), BF),
        grid=(8,),
        in_specs=[
            pl.BlockSpec((1, 1, 256), lambda i: (i, 0, 0)),
            pl.BlockSpec((192, rows), lambda i: (0, 0)),
        ],
        out_specs=pl.BlockSpec((4, 96, 128), lambda i: (i, 0, 0)),
        compiler_params=pltpu.CompilerParams(vmem_limit_bytes=VMEM_LIMIT),
        name="gather_rows",
    )(index, table)


def mixing_kernel(key_ref, out_ref):
    for block in range(8):
        slot = lax.broadcasted_iota(jnp.int16, (128, 128), 0)
        key = (key_ref[...] - 128 * block).astype(jnp.int16)
        total = jnp.zeros((128, 128), BF)
        for k in range(32):
            total = total + jnp.where(slot == key[k : k + 1, :], jnp.ones((), BF), jnp.zeros((), BF))
        out_ref[128 * block : 128 * block + 128, :] = total


def make_mixing(keys):
    return pl.pallas_call(
        mixing_kernel,
        out_shape=jax.ShapeDtypeStruct((1024, 128), BF),
        name="make_mixing",
    )(keys)


def virtual_kernel(rows_ref, mix_ref, *refs):
    own_ref, other_ref = refs[-2:]
    mix = mix_ref[...]
    first = tn(mix, rows_ref[:, 0:32, :].reshape(1024, 128))
    second = tn(mix, rows_ref[:, 32:64, :].reshape(1024, 128))
    both = tn(mix, rows_ref[:, 64:96, :].reshape(1024, 128))
    own_ref[:, 0:128] = first[0:64]
    own_ref[:, 128:192] = both[0:64, 0:64]
    other_ref[:, 0:128] = second[64:128]
    other_ref[:, 128:192] = both[64:128, 64:128]


def mix_rows(rows, mix, *after):
    part = jax.ShapeDtypeStruct((64, 192), F32)
    whole = pl.BlockSpec(memory_space=pltpu.VMEM)
    return pl.pallas_call(
        virtual_kernel,
        out_shape=(part, part),
        in_specs=[whole, whole] + [pl.BlockSpec(memory_space=pl.ANY)] * len(after),
        name="mix_rows",
    )(rows, mix, *after)


def project_kernel(tok_ref, wq_ref, wk_ref, wv_ref, q_ref, k_ref, v_ref):
    tok = tok_ref[...]
    q_ref[...] = nt(tok, wq_ref[...]).astype(BF)
    k_ref[...] = nt(tok, wk_ref[...]).astype(BF)
    v_ref[...] = nt(tok, wv_ref[...]).astype(BF)


def project(tokens, wq, wk, wv):
    out = jax.ShapeDtypeStruct((2048, 192), BF)
    weight = pl.BlockSpec((192, 768), lambda i: (0, 0))
    block = pl.BlockSpec((512, 192), lambda i: (i, 0))
    return pl.pallas_call(
        project_kernel,
        out_shape=(out, out, out),
        grid=(4,),
        in_specs=[pl.BlockSpec((512, 768), lambda i: (i, 0)), weight, weight, weight],
        out_specs=(block, block, block),
        compiler_params=pltpu.CompilerParams(vmem_limit_bytes=VMEM_LIMIT),
        name="project",
    )(tokens, wq, wk, wv)


def attend_kernel(
    place_ref, tok_ref, q_ref, k_ref, v_ref, grad_ref, virt_ref, wk_ref, wv_ref, wk4_ref, wv4_ref,
    ctx_ref, keep_ref, give_ref, vg0_ref, vg1_ref, vg2_ref, vg3_ref,
    acc_ref, kvirt_ref, vvirt_ref, dkvirt_ref, dvvirt_ref,
):
    step = pl.program_id(0)
    width = 192

    @pl.when(step == 0)
    def _():
        acc_ref[...] = jnp.zeros_like(acc_ref)
        row = lax.broadcasted_iota(jnp.int32, (512, 64), 0)
        pair = lax.broadcasted_iota(jnp.int32, (512, 64), 1)
        spread = jnp.where((row // 16 == pair // 2) & (row % 16 == pair % 2), 1.0, 0.0).astype(BF)
        virt = virt_ref[...]
        kvirt_ref[...] = nn(spread, nt(virt, wk_ref[...]).astype(BF)).astype(BF)
        vvirt_ref[...] = nn(spread, nt(virt, wv_ref[...]).astype(BF)).astype(BF)

    tok = tok_ref[...]
    head_row = lax.broadcasted_iota(jnp.int32, (width, width), 0) // HD
    head_col = lax.broadcasted_iota(jnp.int32, (width, width), 1) // HD
    blocks = jnp.where(head_row == head_col, 1.0, 0.0).astype(BF)
    valid = lax.broadcasted_iota(jnp.int32, (80, width), 0) < 66
    lane = lax.broadcasted_iota(jnp.int32, (HD, width), 1)

    def heads_of(full):
        return jnp.where(
            lane < 64, full[0:64], jnp.where(lane < 128, full[64:128], full[128:192])
        )

    dqs, dks, dvs = [], [], []
    for i in range(GROUP):
        at = pl.multiple_of((step * GROUP + i) * 16, 16)
        span = slice(64 * i, 64 * i + 64)
        key = jnp.concatenate([k_ref[span, :], kvirt_ref[pl.ds(at, 16), :]], axis=0)
        value = jnp.concatenate([v_ref[span, :], vvirt_ref[pl.ds(at, 16), :]], axis=0)
        query = q_ref[span, :]
        grad = grad_ref[span, :]
        query_blocks = jnp.concatenate([query, query, query], axis=0) * blocks
        grad_blocks = jnp.concatenate([grad, grad, grad], axis=0) * blocks
        scores = jnp.where(valid, nt(key, query_blocks) * 0.125, -1e30)
        top = jnp.max(scores, axis=0, keepdims=True)
        powers = jnp.exp(scores - top)
        powers = jnp.where(valid, powers, 0.0)
        probs = powers * (1.0 / jnp.sum(powers, axis=0, keepdims=True))
        low = probs.astype(BF)
        prob_grads = nt(value, grad_blocks)
        inner = jnp.sum(prob_grads * probs, axis=0, keepdims=True)
        score_low = (probs * (prob_grads - inner) * 0.125).astype(BF)
        ctx_ref[span, :] = heads_of(tn(low, value)).astype(BF)
        dq = heads_of(tn(score_low, key)).astype(BF)
        dv = nn(low, grad_blocks).astype(BF)
        dk = nn(score_low, query_blocks).astype(BF)
        dkvirt_ref[pl.ds(at, 16), :] = dk[64:80]
        dvvirt_ref[pl.ds(at, 16), :] = dv[64:80]
        dqs.append(dq)
        dks.append(dk[0:64])
        dvs.append(dv[0:64])
    acc_ref[0:192, :] += tn(jnp.concatenate(dqs, axis=0), tok)
    acc_ref[192:384, :] += tn(jnp.concatenate(dks, axis=0), tok)
    acc_ref[384:576, :] += tn(jnp.concatenate(dvs, axis=0), tok)

    @pl.when(step == pl.num_programs(0) - 1)
    def _():
        pair = lax.broadcasted_iota(jnp.int32, (64, 512), 0)
        row = lax.broadcasted_iota(jnp.int32, (64, 512), 1)
        collect = jnp.where((row // 16 == pair // 2) & (row % 16 == pair % 2), 1.0, 0.0).astype(BF)
        dk = nn(collect, dkvirt_ref[...]).astype(BF)
        dv = nn(collect, dvvirt_ref[...]).astype(BF)
        virt = virt_ref[...]
        acc_ref[192:384, :] += tn(dk, virt)
        acc_ref[384:576, :] += tn(dv, virt)
        own = place_ref[0]
        for d, ref in enumerate((vg0_ref, vg1_ref, vg2_ref, vg3_ref)):
            at = (own + d) % 4
            ref[...] = (nn(dk, wk4_ref[at]) + nn(dv, wv4_ref[at])).astype(ref.dtype)
        keep_ref[1728:, :] = jnp.zeros((320, 128), F32)
        give_ref[1728:, :] = jnp.zeros((320, 128), BF)
        for core in range(2):
            @pl.when(place_ref[1] == core)
            def _():
                for t in range(3):
                    keep = 3 * core + t
                    give = 3 * (1 - core) + t
                    rows = slice(576 * t, 576 * t + 576)
                    keep_ref[rows, :] = acc_ref[:, 128 * keep : 128 * keep + 128]
                    give_ref[rows, :] = acc_ref[:, 128 * give : 128 * give + 128].astype(BF)


def attend(place, tokens, q, k, v, grads, virtual, wk, wv, wk4, wv4):
    rows = 64 * GROUP
    steps = CENTRES // GROUP
    fixed2 = lambda i: (0, 0)
    fixed3 = lambda i: (0, 0, 0)
    out_shape = (
        jax.ShapeDtypeStruct((2048, 192), BF),
        jax.ShapeDtypeStruct((2048, 128), F32),
        jax.ShapeDtypeStruct((2048, 128), BF),
        jax.ShapeDtypeStruct((64, 192), F32),
        jax.ShapeDtypeStruct((64, 192), BF),
        jax.ShapeDtypeStruct((64, 192), BF),
        jax.ShapeDtypeStruct((64, 192), BF),
    )
    small = pl.BlockSpec((64, 192), fixed2)
    weight = pl.BlockSpec((192, 768), fixed2)
    head = pl.BlockSpec((rows, 192), lambda i: (i, 0))
    half = pl.BlockSpec((2048, 128), fixed2)
    return pl.pallas_call(
        attend_kernel,
        out_shape=out_shape,
        grid=(steps,),
        in_specs=[
            pl.BlockSpec(memory_space=pltpu.SMEM),
            pl.BlockSpec((rows, 768), lambda i: (i, 0)),
            head, head, head, head,
            pl.BlockSpec((64, 768), fixed2),
            weight, weight,
            pl.BlockSpec((4, 192, 192), fixed3),
            pl.BlockSpec((4, 192, 192), fixed3),
        ],
        out_specs=(
            head, half, half,
            small, small, small, small,
        ),
        scratch_shapes=[
            pltpu.VMEM((576, 768), F32),
            pltpu.VMEM((512, 192), BF),
            pltpu.VMEM((512, 192), BF),
            pltpu.VMEM((512, 192), BF),
            pltpu.VMEM((512, 192), BF),
        ],
        compiler_params=pltpu.CompilerParams(vmem_limit_bytes=VMEM_LIMIT),
        name="attend",
    )(place, tokens, q, k, v, grads, virtual, wk, wv, wk4, wv4)


def spread_kernel(own_ref, other_ref, mix_ref, out_ref):
    mix = mix_ref[...]
    zeros = jnp.zeros((64, 192), BF)

    def split(x):
        high = x.astype(BF)
        return high, (x - high.astype(F32)).astype(BF)

    own_high, own_low = split(own_ref[...])
    other_high, other_low = split(other_ref[...])
    stack = lambda a, b: jnp.concatenate([a, b], axis=0)
    own = nn(mix, stack(own_high, zeros)) + nn(mix, stack(own_low, zeros))
    other = nn(mix, stack(zeros, other_high)) + nn(mix, stack(zeros, other_low))
    own = own.astype(BF)
    other = other.astype(BF)
    out_ref[:, 0:32, :] = own[:, 0:128].reshape(CHIPS, 32, 128)
    out_ref[:, 32:64, :] = other[:, 0:128].reshape(CHIPS, 32, 128)
    out_ref[:, 64:96, 0:64] = own[:, 128:192].reshape(CHIPS, 32, 64)
    out_ref[:, 64:96, 64:128] = other[:, 128:192].reshape(CHIPS, 32, 64)


def spread(own, other, mix):
    whole = pl.BlockSpec(memory_space=pltpu.VMEM)
    return pl.pallas_call(
        spread_kernel,
        out_shape=jax.ShapeDtypeStruct((CHIPS, 96, 128), BF),
        in_specs=[whole] * 3,
        name="spread",
    )(own, other, mix)


def total_kernel(pieces_ref, *refs):
    out_ref = refs[-1]
    total = pieces_ref[0].astype(F32)
    for chip in range(1, CHIPS):
        total = total + pieces_ref[chip].astype(F32)
    out_ref[...] = total.astype(BF)


def sum_pieces(pieces, *after):
    return pl.pallas_call(
        total_kernel,
        out_shape=jax.ShapeDtypeStruct((64, 128), BF),
        in_specs=[pl.BlockSpec(memory_space=pltpu.VMEM)]
        + [pl.BlockSpec(memory_space=pl.ANY)] * len(after),
        name="sum_pieces",
    )(pieces, *after)


def assemble(place_ref, mine_ref, theirs_ref, out_refs):
    for piece in range(27):
        dx = (place_ref[2] - piece // 8 + 4) % 4
        dz = (place_ref[3] - piece % 8 + 8) % 8
        out_ref = out_refs[(piece % 9) // 3]
        rows = slice(64 * (piece % 3), 64 * (piece % 3) + 64)
        mine = mine_ref[dx, dz].astype(F32)
        theirs = theirs_ref[dx, dz].astype(F32)
        low = place_ref[1] == 0
        tile = 128 * (piece // 9)
        out_ref[rows, tile : tile + 128] = jnp.where(low, mine, theirs)
        out_ref[rows, 384 + tile : 512 + tile] = jnp.where(low, theirs, mine)


def scatter_kernel(
    place_ref, index_ref, rows_ref, mine_ref, theirs_ref,
    out_ref, wq_ref, wk_ref, wv_ref, turned_ref,
):
    step = pl.program_id(0)

    @pl.when(step == 0)
    def _():
        assemble(place_ref, mine_ref, theirs_ref, (wq_ref, wk_ref, wv_ref))
        for g in range(8):
            chips = slice(4 * g, 4 * g + 4)
            first = rows_ref[chips, 0:32, :].reshape(128, 128).astype(F32).T.astype(BF)
            second = rows_ref[chips, 32:64, :].reshape(128, 128).astype(F32).T.astype(BF)
            both = rows_ref[chips, 64:96, :].reshape(128, 128).astype(F32).T.astype(BF)
            lanes = slice(256 * g, 256 * g + 128)
            more = slice(256 * g + 128, 256 * g + 256)
            turned_ref[0:128, lanes] = first
            turned_ref[128:192, lanes] = both[0:64]
            turned_ref[0:128, more] = second
            turned_ref[128:192, more] = both[64:128]

    row = lax.broadcasted_iota(jnp.int32, (256, 2048), 0) + 256 * step
    select = jnp.where(row == index_ref[...], 1.0, 0.0).astype(BF)
    out_ref[...] = nt(turned_ref[...], select)


def scatter_rows(place, index, rows, mine, theirs):
    weight = jax.ShapeDtypeStruct((192, 768), F32)
    weight_block = pl.BlockSpec((192, 768), lambda i: (0, 0))
    piece_block = pl.BlockSpec((4, 8, 64, 128), lambda i: (0, 0, 0, 0))
    return pl.pallas_call(
        scatter_kernel,
        out_shape=(jax.ShapeDtypeStruct((192, 2048), F32), weight, weight, weight),
        grid=(8,),
        in_specs=[
            pl.BlockSpec(memory_space=pltpu.SMEM),
            pl.BlockSpec((1, 2048), lambda i: (0, 0)),
            pl.BlockSpec((CHIPS, 96, 128), lambda i: (0, 0, 0)),
            piece_block,
            piece_block,
        ],
        out_specs=(
            pl.BlockSpec((192, 256), lambda i: (0, i)), weight_block, weight_block, weight_block
        ),
        scratch_shapes=[pltpu.VMEM((192, 2048), BF)],
        compiler_params=pltpu.CompilerParams(vmem_limit_bytes=VMEM_LIMIT),
        name="scatter_rows",
    )(place, index, rows, mine, theirs)


def layer(tokens, w_query, w_key, w_value, grad_out, owned_cls, send_rows, neigh_slot, neigh_count):
    node = lax.axis_index("nodes")
    core = node % 2
    place = jnp.stack([lax.axis_index("mp"), core, node // 16, node // 2 % 8]).astype(jnp.int32)

    asked = send_rows.reshape(8, 4, 2, 32)
    asked = jnp.where(core == 0, asked, asked[:, :, ::-1])
    index = asked.transpose(0, 2, 1, 3).reshape(8, 1, 256)
    sent = gather_rows(index, owned_cls)

    slots = neigh_slot.reshape(64, 32)
    counts = neigh_count.reshape(64, 1)
    position = lax.broadcasted_iota(jnp.int32, (64, 32), 1)
    slots = jnp.where(position < counts, slots, -1)
    all_slots = jnp.concatenate([slots, core_swap(slots)], axis=0)
    here = (all_slots >= 0) & (((all_slots >> 5) & 1) == core)
    keys = jnp.where(here, (all_slots >> 6) * 32 + (all_slots & 31), -1).T
    mix = make_mixing(keys)

    heads = grad_out.reshape(32, 3, 64, 64).transpose(0, 2, 1, 3).reshape(2048, 192)
    wk4 = w_key.reshape(192, 4, 192).transpose(1, 0, 2)
    wv4 = w_value.reshape(192, 4, 192).transpose(1, 0, 2)

    flat = tokens.reshape(2048, 768)
    q, k, v = project(flat, w_query, w_key, w_value)

    fetched = chip_exchange(sent)
    own_part, other_part = mix_rows(fetched, mix, q, k, v, heads, wk4, wv4)
    divisor = counts.astype(F32)
    local = ((own_part + core_swap(other_part)) / divisor).astype(BF)
    virtual = lax.all_gather(local, "mp", axis=1, tiled=True)

    ctx, keep, give, vg0, vg1, vg2, vg3 = attend(
        place, flat, q, k, v, heads, virtual, w_key, w_value, wk4, wv4
    )
    context = ctx.reshape(32, 64, 3, 64).transpose(0, 2, 1, 3).reshape(32, 3, 4096)

    around = lambda x, d: lax.ppermute(x, "mp", [(i, (i + d) % 4) for i in range(4)])
    moved = [around(vg, d + 1) for d, vg in enumerate((vg1, vg2, vg3))]
    half = (keep + core_swap(give).astype(F32)).astype(BF)
    pieces = chip_exchange(half.reshape(CHIPS, 64, 128))

    shared = (vg0 + moved[0].astype(F32) + moved[1].astype(F32) + moved[2].astype(F32)) / divisor
    outgoing = spread(shared, core_swap(shared), mix)
    total = sum_pieces(pieces, outgoing, context.transpose(1, 0, 2))
    arrived = chip_exchange(outgoing)
    near = jnp.stack([total] + [along(total, 0, d) for d in range(1, 4)])
    across = along(near, 0, 4)
    row = jnp.concatenate([near, across], axis=0)
    mine = jnp.stack([row] + [along(row, d, 0) for d in range(1, 4)])
    theirs = core_swap(mine)
    grad_cls, grad_query, grad_key, grad_value = scatter_rows(
        place, index.reshape(1, 2048), arrived, mine, theirs
    )
    return (context, grad_query, grad_key, grad_value, grad_cls)


def solution(mesh):
    in_specs = (
        P("nodes", None, None),
        P("mp", None),
        P("mp", None),
        P("mp", None),
        P("nodes", "mp", None),
        P("mp", "nodes"),
        P("nodes", None, None),
        P("nodes", None, None),
        P("nodes", None),
    )
    out_specs = (
        P("nodes", "mp", None),
        P("mp", None),
        P("mp", None),
        P("mp", None),
        P("mp", "nodes"),
    )
    return jax.shard_map(layer, mesh=mesh, in_specs=in_specs, out_specs=out_specs, check_vma=False)
```

```python
import jax
import jax.numpy as jnp
from jax import lax
from jax.experimental import pallas as pl
from jax.experimental.pallas import tpu as pltpu
from jax.sharding import PartitionSpec as P


HD = 64
BF = jnp.bfloat16
F32 = jnp.float32
CHIPS = 32
CENTRES = 32
GROUP = 8
VMEM_LIMIT = 60 * 1024 * 1024

XZ_GROUPS = [[chip * 2 + core for chip in range(CHIPS)] for core in range(2)]
CORE_SWAP = [(dev, dev ^ 1) for dev in range(2 * CHIPS)]


def nt(a, b):
    return lax.dot_general(a, b, (((1,), (1,)), ((), ())), preferred_element_type=F32)


def nn(a, b):
    return lax.dot_general(a, b, (((1,), (0,)), ((), ())), preferred_element_type=F32)


def tn(a, b):
    return lax.dot_general(a, b, (((0,), (0,)), ((), ())), preferred_element_type=F32)


def core_swap(x):
    return lax.ppermute(x, "nodes", CORE_SWAP)


def along(x, dx, dz):
    pairs = []
    for dev in range(2 * CHIPS):
        at_x, at_z, core = dev // 16, dev // 2 % 8, dev % 2
        pairs.append((dev, ((at_x + dx) % 4 * 8 + (at_z + dz) % 8) * 2 + core))
    return lax.ppermute(x, "nodes", pairs)


def chip_exchange(x):
    return lax.all_to_all(
        x, "nodes", split_axis=0, concat_axis=0, tiled=True, axis_index_groups=XZ_GROUPS
    )


def gather_kernel(index_ref, table_ref, out_ref):
    rows = table_ref.shape[1]
    row = lax.broadcasted_iota(jnp.int32, (rows, 256), 0)
    select = jnp.where(row == index_ref[0], 1.0, 0.0).astype(BF)
    picked = nn(table_ref[...], select)
    turned = picked.T.astype(BF)
    for chip in range(4):
        own = turned[32 * chip : 32 * chip + 32]
        other = turned[128 + 32 * chip : 160 + 32 * chip]
        out_ref[chip, 0:32, :] = own[:, 0:128]
        out_ref[chip, 32:64, :] = other[:, 0:128]
        out_ref[chip, 64:96, 0:64] = own[:, 128:192]
        out_ref[chip, 64:96, 64:128] = other[:, 128:192]


def gather_rows(index, table):
    rows = table.shape[1]
    return pl.pallas_call(
        gather_kernel,
        out_shape=jax.ShapeDtypeStruct((CHIPS, 96, 128), BF),
        grid=(8,),
        in_specs=[
            pl.BlockSpec((1, 1, 256), lambda i: (i, 0, 0)),
            pl.BlockSpec((192, rows), lambda i: (0, 0)),
        ],
        out_specs=pl.BlockSpec((4, 96, 128), lambda i: (i, 0, 0)),
        compiler_params=pltpu.CompilerParams(vmem_limit_bytes=VMEM_LIMIT),
        name="gather_rows",
    )(index, table)


def mixing_kernel(key_ref, out_ref):
    for block in range(8):
        slot = lax.broadcasted_iota(jnp.int16, (128, 128), 0)
        key = (key_ref[...] - 128 * block).astype(jnp.int16)
        total = jnp.zeros((128, 128), BF)
        for k in range(32):
            total = total + jnp.where(slot == key[k : k + 1, :], jnp.ones((), BF), jnp.zeros((), BF))
        out_ref[128 * block : 128 * block + 128, :] = total


def make_mixing(keys):
    return pl.pallas_call(
        mixing_kernel,
        out_shape=jax.ShapeDtypeStruct((1024, 128), BF),
        name="make_mixing",
    )(keys)


def virtual_kernel(rows_ref, mix_ref, *refs):
    own_ref, other_ref = refs[-2:]
    mix = mix_ref[...]
    first = tn(mix, rows_ref[:, 0:32, :].reshape(1024, 128))
    second = tn(mix, rows_ref[:, 32:64, :].reshape(1024, 128))
    both = tn(mix, rows_ref[:, 64:96, :].reshape(1024, 128))
    own_ref[:, 0:128] = first[0:64]
    own_ref[:, 128:192] = both[0:64, 0:64]
    other_ref[:, 0:128] = second[64:128]
    other_ref[:, 128:192] = both[64:128, 64:128]


def mix_rows(rows, mix, *after):
    part = jax.ShapeDtypeStruct((64, 192), F32)
    whole = pl.BlockSpec(memory_space=pltpu.VMEM)
    return pl.pallas_call(
        virtual_kernel,
        out_shape=(part, part),
        in_specs=[whole, whole] + [pl.BlockSpec(memory_space=pl.ANY)] * len(after),
        name="mix_rows",
    )(rows, mix, *after)


def project_kernel(tok_ref, wq_ref, wk_ref, wv_ref, q_ref, k_ref, v_ref):
    tok = tok_ref[...]
    q_ref[...] = nt(tok, wq_ref[...]).astype(BF)
    k_ref[...] = nt(tok, wk_ref[...]).astype(BF)
    v_ref[...] = nt(tok, wv_ref[...]).astype(BF)


def project(tokens, wq, wk, wv):
    out = jax.ShapeDtypeStruct((2048, 192), BF)
    weight = pl.BlockSpec((192, 768), lambda i: (0, 0))
    block = pl.BlockSpec((512, 192), lambda i: (i, 0))
    return pl.pallas_call(
        project_kernel,
        out_shape=(out, out, out),
        grid=(4,),
        in_specs=[pl.BlockSpec((512, 768), lambda i: (i, 0)), weight, weight, weight],
        out_specs=(block, block, block),
        compiler_params=pltpu.CompilerParams(vmem_limit_bytes=VMEM_LIMIT),
        name="project",
    )(tokens, wq, wk, wv)


def attend_kernel(
    place_ref, tok_ref, q_ref, k_ref, v_ref, grad_ref, virt_ref, wk_ref, wv_ref, wk4_ref, wv4_ref,
    ctx_ref, keep_ref, give_ref, vg0_ref, vg1_ref, vg2_ref, vg3_ref,
    acc_ref, kvirt_ref, vvirt_ref, dkvirt_ref, dvvirt_ref,
):
    step = pl.program_id(0)
    width = 192

    @pl.when(step == 0)
    def _():
        acc_ref[...] = jnp.zeros_like(acc_ref)
        row = lax.broadcasted_iota(jnp.int32, (512, 64), 0)
        pair = lax.broadcasted_iota(jnp.int32, (512, 64), 1)
        spread = jnp.where((row // 16 == pair // 2) & (row % 16 == pair % 2), 1.0, 0.0).astype(BF)
        virt = virt_ref[...]
        kvirt_ref[...] = nn(spread, nt(virt, wk_ref[...]).astype(BF)).astype(BF)
        vvirt_ref[...] = nn(spread, nt(virt, wv_ref[...]).astype(BF)).astype(BF)

    tok = tok_ref[...]
    head_row = lax.broadcasted_iota(jnp.int32, (width, width), 0) // HD
    head_col = lax.broadcasted_iota(jnp.int32, (width, width), 1) // HD
    blocks = jnp.where(head_row == head_col, 1.0, 0.0).astype(BF)
    valid = lax.broadcasted_iota(jnp.int32, (80, width), 0) < 66
    lane = lax.broadcasted_iota(jnp.int32, (HD, width), 1)

    def heads_of(full):
        return jnp.where(
            lane < 64, full[0:64], jnp.where(lane < 128, full[64:128], full[128:192])
        )

    empty = jnp.zeros((HD, HD), BF)
    dqs, dks, dvs = [], [], []
    for i in range(GROUP):
        at = pl.multiple_of((step * GROUP + i) * 16, 16)
        span = slice(64 * i, 64 * i + 64)
        key = jnp.concatenate([k_ref[span, :], kvirt_ref[pl.ds(at, 16), :]], axis=0)
        value = jnp.concatenate([v_ref[span, :], vvirt_ref[pl.ds(at, 16), :]], axis=0)
        query = q_ref[span, :]
        first, second, third = grad_ref[0, span, :], grad_ref[1, span, :], grad_ref[2, span, :]
        query_blocks = jnp.concatenate([query, query, query], axis=0) * blocks
        grad_blocks = jnp.concatenate(
            [
                jnp.concatenate([first, empty, empty], axis=1),
                jnp.concatenate([empty, second, empty], axis=1),
                jnp.concatenate([empty, empty, third], axis=1),
            ],
            axis=0,
        )
        scores = jnp.where(valid, nt(key, query_blocks) * 0.125, -1e30)
        top = jnp.max(scores, axis=0, keepdims=True)
        powers = jnp.exp(scores - top)
        powers = jnp.where(valid, powers, 0.0)
        probs = powers * (1.0 / jnp.sum(powers, axis=0, keepdims=True))
        low = probs.astype(BF)
        prob_grads = nt(value, grad_blocks)
        inner = jnp.sum(prob_grads * probs, axis=0, keepdims=True)
        score_low = (probs * (prob_grads - inner) * 0.125).astype(BF)
        mixed = tn(low, value)
        for h in range(3):
            part = slice(HD * h, HD * h + HD)
            ctx_ref[h, span, :] = mixed[part, part].astype(BF)
        dq = heads_of(tn(score_low, key)).astype(BF)
        dv = nn(low, grad_blocks).astype(BF)
        dk = nn(score_low, query_blocks).astype(BF)
        dkvirt_ref[pl.ds(at, 16), :] = dk[64:80]
        dvvirt_ref[pl.ds(at, 16), :] = dv[64:80]
        dqs.append(dq)
        dks.append(dk[0:64])
        dvs.append(dv[0:64])
    acc_ref[0:192, :] += tn(jnp.concatenate(dqs, axis=0), tok)
    acc_ref[192:384, :] += tn(jnp.concatenate(dks, axis=0), tok)
    acc_ref[384:576, :] += tn(jnp.concatenate(dvs, axis=0), tok)

    @pl.when(step == pl.num_programs(0) - 1)
    def _():
        pair = lax.broadcasted_iota(jnp.int32, (64, 512), 0)
        row = lax.broadcasted_iota(jnp.int32, (64, 512), 1)
        collect = jnp.where((row // 16 == pair // 2) & (row % 16 == pair % 2), 1.0, 0.0).astype(BF)
        dk = nn(collect, dkvirt_ref[...]).astype(BF)
        dv = nn(collect, dvvirt_ref[...]).astype(BF)
        virt = virt_ref[...]
        acc_ref[192:384, :] += tn(dk, virt)
        acc_ref[384:576, :] += tn(dv, virt)
        own = place_ref[0]
        for d, ref in enumerate((vg0_ref, vg1_ref, vg2_ref, vg3_ref)):
            at = (own + d) % 4
            ref[...] = (nn(dk, wk4_ref[at]) + nn(dv, wv4_ref[at])).astype(ref.dtype)
        keep_ref[1728:, :] = jnp.zeros((320, 128), F32)
        give_ref[1728:, :] = jnp.zeros((320, 128), BF)
        for core in range(2):
            @pl.when(place_ref[1] == core)
            def _():
                for t in range(3):
                    keep = 3 * core + t
                    give = 3 * (1 - core) + t
                    rows = slice(576 * t, 576 * t + 576)
                    keep_ref[rows, :] = acc_ref[:, 128 * keep : 128 * keep + 128]
                    give_ref[rows, :] = acc_ref[:, 128 * give : 128 * give + 128].astype(BF)


def attend(place, tokens, q, k, v, grads, virtual, wk, wv, wk4, wv4):
    rows = 64 * GROUP
    steps = CENTRES // GROUP
    fixed2 = lambda i: (0, 0)
    fixed3 = lambda i: (0, 0, 0)
    out_shape = (
        jax.ShapeDtypeStruct((3, 2048, HD), BF),
        jax.ShapeDtypeStruct((2048, 128), F32),
        jax.ShapeDtypeStruct((2048, 128), BF),
        jax.ShapeDtypeStruct((64, 192), F32),
        jax.ShapeDtypeStruct((64, 192), BF),
        jax.ShapeDtypeStruct((64, 192), BF),
        jax.ShapeDtypeStruct((64, 192), BF),
    )
    small = pl.BlockSpec((64, 192), fixed2)
    weight = pl.BlockSpec((192, 768), fixed2)
    head = pl.BlockSpec((rows, 192), lambda i: (i, 0))
    by_head = pl.BlockSpec((3, rows, HD), lambda i: (0, i, 0))
    half = pl.BlockSpec((2048, 128), fixed2)
    return pl.pallas_call(
        attend_kernel,
        out_shape=out_shape,
        grid=(steps,),
        in_specs=[
            pl.BlockSpec(memory_space=pltpu.SMEM),
            pl.BlockSpec((rows, 768), lambda i: (i, 0)),
            head, head, head, by_head,
            pl.BlockSpec((64, 768), fixed2),
            weight, weight,
            pl.BlockSpec((4, 192, 192), fixed3),
            pl.BlockSpec((4, 192, 192), fixed3),
        ],
        out_specs=(
            by_head, half, half,
            small, small, small, small,
        ),
        scratch_shapes=[
            pltpu.VMEM((576, 768), F32),
            pltpu.VMEM((512, 192), BF),
            pltpu.VMEM((512, 192), BF),
            pltpu.VMEM((512, 192), BF),
            pltpu.VMEM((512, 192), BF),
        ],
        compiler_params=pltpu.CompilerParams(vmem_limit_bytes=VMEM_LIMIT),
        name="attend",
    )(place, tokens, q, k, v, grads, virtual, wk, wv, wk4, wv4)


def spread_kernel(own_ref, other_ref, mix_ref, out_ref):
    mix = mix_ref[...]
    zeros = jnp.zeros((64, 192), BF)

    def split(x):
        high = x.astype(BF)
        return high, (x - high.astype(F32)).astype(BF)

    own_high, own_low = split(own_ref[...])
    other_high, other_low = split(other_ref[...])
    stack = lambda a, b: jnp.concatenate([a, b], axis=0)
    own = nn(mix, stack(own_high, zeros)) + nn(mix, stack(own_low, zeros))
    other = nn(mix, stack(zeros, other_high)) + nn(mix, stack(zeros, other_low))
    own = own.astype(BF)
    other = other.astype(BF)
    out_ref[:, 0:32, :] = own[:, 0:128].reshape(CHIPS, 32, 128)
    out_ref[:, 32:64, :] = other[:, 0:128].reshape(CHIPS, 32, 128)
    out_ref[:, 64:96, 0:64] = own[:, 128:192].reshape(CHIPS, 32, 64)
    out_ref[:, 64:96, 64:128] = other[:, 128:192].reshape(CHIPS, 32, 64)


def spread(own, other, mix):
    whole = pl.BlockSpec(memory_space=pltpu.VMEM)
    return pl.pallas_call(
        spread_kernel,
        out_shape=jax.ShapeDtypeStruct((CHIPS, 96, 128), BF),
        in_specs=[whole] * 3,
        name="spread",
    )(own, other, mix)


def total_kernel(pieces_ref, *refs):
    out_ref = refs[-1]
    total = pieces_ref[0].astype(F32)
    for chip in range(1, CHIPS):
        total = total + pieces_ref[chip].astype(F32)
    out_ref[...] = total.astype(BF)


def sum_pieces(pieces, *after):
    return pl.pallas_call(
        total_kernel,
        out_shape=jax.ShapeDtypeStruct((64, 128), BF),
        in_specs=[pl.BlockSpec(memory_space=pltpu.VMEM)]
        + [pl.BlockSpec(memory_space=pl.ANY)] * len(after),
        name="sum_pieces",
    )(pieces, *after)


def assemble(place_ref, mine_ref, theirs_ref, out_refs):
    for piece in range(27):
        dx = (place_ref[2] - piece // 8 + 4) % 4
        dz = (place_ref[3] - piece % 8 + 8) % 8
        out_ref = out_refs[(piece % 9) // 3]
        rows = slice(64 * (piece % 3), 64 * (piece % 3) + 64)
        mine = mine_ref[dx, dz].astype(F32)
        theirs = theirs_ref[dx, dz].astype(F32)
        low = place_ref[1] == 0
        tile = 128 * (piece // 9)
        out_ref[rows, tile : tile + 128] = jnp.where(low, mine, theirs)
        out_ref[rows, 384 + tile : 512 + tile] = jnp.where(low, theirs, mine)


def scatter_kernel(
    place_ref, index_ref, rows_ref, mine_ref, theirs_ref,
    out_ref, wq_ref, wk_ref, wv_ref, turned_ref,
):
    step = pl.program_id(0)

    @pl.when(step == 0)
    def _():
        assemble(place_ref, mine_ref, theirs_ref, (wq_ref, wk_ref, wv_ref))
        for g in range(8):
            chips = slice(4 * g, 4 * g + 4)
            first = rows_ref[chips, 0:32, :].reshape(128, 128).astype(F32).T.astype(BF)
            second = rows_ref[chips, 32:64, :].reshape(128, 128).astype(F32).T.astype(BF)
            both = rows_ref[chips, 64:96, :].reshape(128, 128).astype(F32).T.astype(BF)
            lanes = slice(256 * g, 256 * g + 128)
            more = slice(256 * g + 128, 256 * g + 256)
            turned_ref[0:128, lanes] = first
            turned_ref[128:192, lanes] = both[0:64]
            turned_ref[0:128, more] = second
            turned_ref[128:192, more] = both[64:128]

    row = lax.broadcasted_iota(jnp.int32, (256, 2048), 0) + 256 * step
    select = jnp.where(row == index_ref[...], 1.0, 0.0).astype(BF)
    out_ref[...] = nt(turned_ref[...], select)


def scatter_rows(place, index, rows, mine, theirs):
    weight = jax.ShapeDtypeStruct((192, 768), F32)
    weight_block = pl.BlockSpec((192, 768), lambda i: (0, 0))
    piece_block = pl.BlockSpec((4, 8, 64, 128), lambda i: (0, 0, 0, 0))
    return pl.pallas_call(
        scatter_kernel,
        out_shape=(jax.ShapeDtypeStruct((192, 2048), F32), weight, weight, weight),
        grid=(8,),
        in_specs=[
            pl.BlockSpec(memory_space=pltpu.SMEM),
            pl.BlockSpec((1, 2048), lambda i: (0, 0)),
            pl.BlockSpec((CHIPS, 96, 128), lambda i: (0, 0, 0)),
            piece_block,
            piece_block,
        ],
        out_specs=(
            pl.BlockSpec((192, 256), lambda i: (0, i)), weight_block, weight_block, weight_block
        ),
        scratch_shapes=[pltpu.VMEM((192, 2048), BF)],
        compiler_params=pltpu.CompilerParams(vmem_limit_bytes=VMEM_LIMIT),
        name="scatter_rows",
    )(place, index, rows, mine, theirs)


def layer(tokens, w_query, w_key, w_value, grad_out, owned_cls, send_rows, neigh_slot, neigh_count):
    node = lax.axis_index("nodes")
    core = node % 2
    place = jnp.stack([lax.axis_index("mp"), core, node // 16, node // 2 % 8]).astype(jnp.int32)

    asked = send_rows.reshape(8, 4, 2, 32)
    asked = jnp.where(core == 0, asked, asked[:, :, ::-1])
    index = asked.transpose(0, 2, 1, 3).reshape(8, 1, 256)
    sent = gather_rows(index, owned_cls)

    slots = neigh_slot.reshape(64, 32)
    counts = neigh_count.reshape(64, 1)
    position = lax.broadcasted_iota(jnp.int32, (64, 32), 1)
    slots = jnp.where(position < counts, slots, -1)
    all_slots = jnp.concatenate([slots, core_swap(slots)], axis=0)
    here = (all_slots >= 0) & (((all_slots >> 5) & 1) == core)
    keys = jnp.where(here, (all_slots >> 6) * 32 + (all_slots & 31), -1).T
    mix = make_mixing(keys)

    heads = grad_out.transpose(1, 0, 2).reshape(3, 2048, HD)
    wk4 = w_key.reshape(192, 4, 192).transpose(1, 0, 2)
    wv4 = w_value.reshape(192, 4, 192).transpose(1, 0, 2)

    flat = tokens.reshape(2048, 768)
    q, k, v = project(flat, w_query, w_key, w_value)

    fetched = chip_exchange(sent)
    own_part, other_part = mix_rows(fetched, mix, q, k, v, heads, wk4, wv4)
    divisor = counts.astype(F32)
    local = ((own_part + core_swap(other_part)) / divisor).astype(BF)
    virtual = lax.all_gather(local, "mp", axis=1, tiled=True)

    ctx, keep, give, vg0, vg1, vg2, vg3 = attend(
        place, flat, q, k, v, heads, virtual, w_key, w_value, wk4, wv4
    )
    context = ctx.reshape(3, 32, 4096).transpose(1, 0, 2)

    around = lambda x, d: lax.ppermute(x, "mp", [(i, (i + d) % 4) for i in range(4)])
    moved = [around(vg, d + 1) for d, vg in enumerate((vg1, vg2, vg3))]
    half = (keep + core_swap(give).astype(F32)).astype(BF)
    pieces = chip_exchange(half.reshape(CHIPS, 64, 128))

    shared = (vg0 + moved[0].astype(F32) + moved[1].astype(F32) + moved[2].astype(F32)) / divisor
    outgoing = spread(shared, core_swap(shared), mix)
    total = sum_pieces(pieces, outgoing, context.transpose(1, 0, 2))
    arrived = chip_exchange(outgoing)
    near = jnp.stack([total] + [along(total, 0, d) for d in range(1, 4)])
    across = along(near, 0, 4)
    row = jnp.concatenate([near, across], axis=0)
    mine = jnp.stack([row] + [along(row, d, 0) for d in range(1, 4)])
    theirs = core_swap(mine)
    grad_cls, grad_query, grad_key, grad_value = scatter_rows(
        place, index.reshape(1, 2048), arrived, mine, theirs
    )
    return (context, grad_query, grad_key, grad_value, grad_cls)


def solution(mesh):
    in_specs = (
        P("nodes", None, None),
        P("mp", None),
        P("mp", None),
        P("mp", None),
        P("nodes", "mp", None),
        P("mp", "nodes"),
        P("nodes", None, None),
        P("nodes", None, None),
        P("nodes", None),
    )
    out_specs = (
        P("nodes", "mp", None),
        P("mp", None),
        P("mp", None),
        P("mp", None),
        P("mp", "nodes"),
    )
    return jax.shard_map(layer, mesh=mesh, in_specs=in_specs, out_specs=out_specs, check_vma=False)
```

```python
import jax
import jax.numpy as jnp
from jax import lax
from jax.experimental import pallas as pl
from jax.experimental.pallas import tpu as pltpu
from jax.sharding import PartitionSpec as P


HD = 64
BF = jnp.bfloat16
F32 = jnp.float32
CHIPS = 32
CENTRES = 32
GROUP = 8
VMEM_LIMIT = 60 * 1024 * 1024

XZ_GROUPS = [[chip * 2 + core for chip in range(CHIPS)] for core in range(2)]
CORE_SWAP = [(dev, dev ^ 1) for dev in range(2 * CHIPS)]


def nt(a, b):
    return lax.dot_general(a, b, (((1,), (1,)), ((), ())), preferred_element_type=F32)


def nn(a, b):
    return lax.dot_general(a, b, (((1,), (0,)), ((), ())), preferred_element_type=F32)


def tn(a, b):
    return lax.dot_general(a, b, (((0,), (0,)), ((), ())), preferred_element_type=F32)


def near(x):
    return pltpu.with_memory_space_constraint(x, pltpu.VMEM)


def core_swap(x):
    return lax.ppermute(x, "nodes", CORE_SWAP)


def along(x, dx, dz):
    pairs = []
    for dev in range(2 * CHIPS):
        at_x, at_z, core = dev // 16, dev // 2 % 8, dev % 2
        pairs.append((dev, ((at_x + dx) % 4 * 8 + (at_z + dz) % 8) * 2 + core))
    return lax.ppermute(x, "nodes", pairs)


def chip_exchange(x):
    return lax.all_to_all(
        x, "nodes", split_axis=0, concat_axis=0, tiled=True, axis_index_groups=XZ_GROUPS
    )


def gather_kernel(index_ref, table_ref, out_ref):
    rows = table_ref.shape[1]
    row = lax.broadcasted_iota(jnp.int32, (rows, 256), 0)
    select = jnp.where(row == index_ref[0], 1.0, 0.0).astype(BF)
    picked = nn(table_ref[...], select)
    turned = picked.T.astype(BF)
    for chip in range(4):
        own = turned[32 * chip : 32 * chip + 32]
        other = turned[128 + 32 * chip : 160 + 32 * chip]
        out_ref[chip, 0:32, :] = own[:, 0:128]
        out_ref[chip, 32:64, :] = other[:, 0:128]
        out_ref[chip, 64:96, 0:64] = own[:, 128:192]
        out_ref[chip, 64:96, 64:128] = other[:, 128:192]


def gather_rows(index, table):
    rows = table.shape[1]
    return pl.pallas_call(
        gather_kernel,
        out_shape=jax.ShapeDtypeStruct((CHIPS, 96, 128), BF),
        grid=(8,),
        in_specs=[
            pl.BlockSpec((1, 1, 256), lambda i: (i, 0, 0)),
            pl.BlockSpec((192, rows), lambda i: (0, 0)),
        ],
        out_specs=pl.BlockSpec((4, 96, 128), lambda i: (i, 0, 0)),
        compiler_params=pltpu.CompilerParams(vmem_limit_bytes=VMEM_LIMIT),
        name="gather_rows",
    )(index, table)


def mixing_kernel(key_ref, out_ref):
    for block in range(8):
        slot = lax.broadcasted_iota(jnp.int16, (128, 128), 0)
        key = (key_ref[...] - 128 * block).astype(jnp.int16)
        total = jnp.zeros((128, 128), BF)
        for k in range(32):
            total = total + jnp.where(slot == key[k : k + 1, :], jnp.ones((), BF), jnp.zeros((), BF))
        out_ref[128 * block : 128 * block + 128, :] = total


def make_mixing(keys):
    return pl.pallas_call(
        mixing_kernel,
        out_shape=jax.ShapeDtypeStruct((1024, 128), BF),
        name="make_mixing",
    )(keys)


def virtual_kernel(rows_ref, mix_ref, *refs):
    own_ref, other_ref = refs[-2:]
    mix = mix_ref[...]
    first = tn(mix, rows_ref[:, 0:32, :].reshape(1024, 128))
    second = tn(mix, rows_ref[:, 32:64, :].reshape(1024, 128))
    both = tn(mix, rows_ref[:, 64:96, :].reshape(1024, 128))
    own_ref[:, 0:128] = first[0:64]
    own_ref[:, 128:192] = both[0:64, 0:64]
    other_ref[:, 0:128] = second[64:128]
    other_ref[:, 128:192] = both[64:128, 64:128]


def mix_rows(rows, mix, *after):
    part = jax.ShapeDtypeStruct((64, 192), F32)
    whole = pl.BlockSpec(memory_space=pltpu.VMEM)
    return pl.pallas_call(
        virtual_kernel,
        out_shape=(part, part),
        in_specs=[whole, whole] + [pl.BlockSpec(memory_space=pl.ANY)] * len(after),
        name="mix_rows",
    )(near(rows), mix, *after)


def project_kernel(tok_ref, wq_ref, wk_ref, wv_ref, q_ref, k_ref, v_ref):
    tok = tok_ref[...]
    q_ref[...] = nt(tok, wq_ref[...]).astype(BF)
    k_ref[...] = nt(tok, wk_ref[...]).astype(BF)
    v_ref[...] = nt(tok, wv_ref[...]).astype(BF)


def project(tokens, wq, wk, wv):
    out = jax.ShapeDtypeStruct((2048, 192), BF)
    weight = pl.BlockSpec((192, 768), lambda i: (0, 0))
    block = pl.BlockSpec((512, 192), lambda i: (i, 0))
    return pl.pallas_call(
        project_kernel,
        out_shape=(out, out, out),
        grid=(4,),
        in_specs=[pl.BlockSpec((512, 768), lambda i: (i, 0)), weight, weight, weight],
        out_specs=(block, block, block),
        compiler_params=pltpu.CompilerParams(vmem_limit_bytes=VMEM_LIMIT),
        name="project",
    )(tokens, wq, wk, wv)


def attend_kernel(
    place_ref, tok_ref, q_ref, k_ref, v_ref, grad_ref, virt_ref, wk_ref, wv_ref, wk4_ref, wv4_ref,
    ctx_ref, keep_ref, give_ref, vg0_ref, vg1_ref, vg2_ref, vg3_ref,
    acc_ref, kvirt_ref, vvirt_ref, dkvirt_ref, dvvirt_ref,
):
    step = pl.program_id(0)
    width = 192

    @pl.when(step == 0)
    def _():
        acc_ref[...] = jnp.zeros_like(acc_ref)
        row = lax.broadcasted_iota(jnp.int32, (512, 64), 0)
        pair = lax.broadcasted_iota(jnp.int32, (512, 64), 1)
        spread = jnp.where((row // 16 == pair // 2) & (row % 16 == pair % 2), 1.0, 0.0).astype(BF)
        virt = virt_ref[...]
        kvirt_ref[...] = nn(spread, nt(virt, wk_ref[...]).astype(BF)).astype(BF)
        vvirt_ref[...] = nn(spread, nt(virt, wv_ref[...]).astype(BF)).astype(BF)

    tok = tok_ref[...]
    head_row = lax.broadcasted_iota(jnp.int32, (width, width), 0) // HD
    head_col = lax.broadcasted_iota(jnp.int32, (width, width), 1) // HD
    blocks = jnp.where(head_row == head_col, 1.0, 0.0).astype(BF)
    valid = lax.broadcasted_iota(jnp.int32, (80, width), 0) < 66
    lane = lax.broadcasted_iota(jnp.int32, (HD, width), 1)

    def heads_of(full):
        return jnp.where(
            lane < 64, full[0:64], jnp.where(lane < 128, full[64:128], full[128:192])
        )

    empty = jnp.zeros((HD, HD), BF)
    dqs, dks, dvs = [], [], []
    for i in range(GROUP):
        at = pl.multiple_of((step * GROUP + i) * 16, 16)
        span = slice(64 * i, 64 * i + 64)
        key = jnp.concatenate([k_ref[span, :], kvirt_ref[pl.ds(at, 16), :]], axis=0)
        value = jnp.concatenate([v_ref[span, :], vvirt_ref[pl.ds(at, 16), :]], axis=0)
        query = q_ref[span, :]
        first, second, third = grad_ref[0, span, :], grad_ref[1, span, :], grad_ref[2, span, :]
        query_blocks = jnp.concatenate([query, query, query], axis=0) * blocks
        grad_blocks = jnp.concatenate(
            [
                jnp.concatenate([first, empty, empty], axis=1),
                jnp.concatenate([empty, second, empty], axis=1),
                jnp.concatenate([empty, empty, third], axis=1),
            ],
            axis=0,
        )
        scores = jnp.where(valid, nt(key, query_blocks) * 0.125, -1e30)
        top = jnp.max(scores, axis=0, keepdims=True)
        powers = jnp.exp(scores - top)
        powers = jnp.where(valid, powers, 0.0)
        probs = powers * (1.0 / jnp.sum(powers, axis=0, keepdims=True))
        low = probs.astype(BF)
        prob_grads = nt(value, grad_blocks)
        inner = jnp.sum(prob_grads * probs, axis=0, keepdims=True)
        score_low = (probs * (prob_grads - inner) * 0.125).astype(BF)
        mixed = tn(low, value)
        for h in range(3):
            part = slice(HD * h, HD * h + HD)
            ctx_ref[h, span, :] = mixed[part, part].astype(BF)
        dq = heads_of(tn(score_low, key)).astype(BF)
        dv = nn(low, grad_blocks).astype(BF)
        dk = nn(score_low, query_blocks).astype(BF)
        dkvirt_ref[pl.ds(at, 16), :] = dk[64:80]
        dvvirt_ref[pl.ds(at, 16), :] = dv[64:80]
        dqs.append(dq)
        dks.append(dk[0:64])
        dvs.append(dv[0:64])
    acc_ref[0:192, :] += tn(jnp.concatenate(dqs, axis=0), tok)
    acc_ref[192:384, :] += tn(jnp.concatenate(dks, axis=0), tok)
    acc_ref[384:576, :] += tn(jnp.concatenate(dvs, axis=0), tok)

    @pl.when(step == pl.num_programs(0) - 1)
    def _():
        pair = lax.broadcasted_iota(jnp.int32, (64, 512), 0)
        row = lax.broadcasted_iota(jnp.int32, (64, 512), 1)
        collect = jnp.where((row // 16 == pair // 2) & (row % 16 == pair % 2), 1.0, 0.0).astype(BF)
        dk = nn(collect, dkvirt_ref[...]).astype(BF)
        dv = nn(collect, dvvirt_ref[...]).astype(BF)
        virt = virt_ref[...]
        acc_ref[192:384, :] += tn(dk, virt)
        acc_ref[384:576, :] += tn(dv, virt)
        own = place_ref[0]
        for d, ref in enumerate((vg0_ref, vg1_ref, vg2_ref, vg3_ref)):
            at = (own + d) % 4
            ref[...] = (nn(dk, wk4_ref[at]) + nn(dv, wv4_ref[at])).astype(ref.dtype)
        keep_ref[1728:, :] = jnp.zeros((320, 128), F32)
        give_ref[1728:, :] = jnp.zeros((320, 128), BF)
        for core in range(2):
            @pl.when(place_ref[1] == core)
            def _():
                for t in range(3):
                    keep = 3 * core + t
                    give = 3 * (1 - core) + t
                    rows = slice(576 * t, 576 * t + 576)
                    keep_ref[rows, :] = acc_ref[:, 128 * keep : 128 * keep + 128]
                    give_ref[rows, :] = acc_ref[:, 128 * give : 128 * give + 128].astype(BF)


def attend(place, tokens, q, k, v, grads, virtual, wk, wv, wk4, wv4):
    rows = 64 * GROUP
    steps = CENTRES // GROUP
    fixed2 = lambda i: (0, 0)
    fixed3 = lambda i: (0, 0, 0)
    out_shape = (
        jax.ShapeDtypeStruct((3, 2048, HD), BF),
        jax.ShapeDtypeStruct((2048, 128), F32),
        jax.ShapeDtypeStruct((2048, 128), BF),
        jax.ShapeDtypeStruct((64, 192), F32),
        jax.ShapeDtypeStruct((64, 192), BF),
        jax.ShapeDtypeStruct((64, 192), BF),
        jax.ShapeDtypeStruct((64, 192), BF),
    )
    small = pl.BlockSpec((64, 192), fixed2)
    weight = pl.BlockSpec((192, 768), fixed2)
    head = pl.BlockSpec((rows, 192), lambda i: (i, 0))
    by_head = pl.BlockSpec((3, rows, HD), lambda i: (0, i, 0))
    half = pl.BlockSpec((2048, 128), fixed2)
    return pl.pallas_call(
        attend_kernel,
        out_shape=out_shape,
        grid=(steps,),
        in_specs=[
            pl.BlockSpec(memory_space=pltpu.SMEM),
            pl.BlockSpec((rows, 768), lambda i: (i, 0)),
            head, head, head, by_head,
            pl.BlockSpec((64, 768), fixed2),
            weight, weight,
            pl.BlockSpec((4, 192, 192), fixed3),
            pl.BlockSpec((4, 192, 192), fixed3),
        ],
        out_specs=(
            by_head, half, half,
            small, small, small, small,
        ),
        scratch_shapes=[
            pltpu.VMEM((576, 768), F32),
            pltpu.VMEM((512, 192), BF),
            pltpu.VMEM((512, 192), BF),
            pltpu.VMEM((512, 192), BF),
            pltpu.VMEM((512, 192), BF),
        ],
        compiler_params=pltpu.CompilerParams(vmem_limit_bytes=VMEM_LIMIT),
        name="attend",
    )(place, tokens, q, k, v, grads, virtual, wk, wv, wk4, wv4)


def spread_kernel(own_ref, other_ref, mix_ref, out_ref):
    mix = mix_ref[...]
    zeros = jnp.zeros((64, 192), BF)

    def split(x):
        high = x.astype(BF)
        return high, (x - high.astype(F32)).astype(BF)

    own_high, own_low = split(own_ref[...])
    other_high, other_low = split(other_ref[...])
    stack = lambda a, b: jnp.concatenate([a, b], axis=0)
    own = nn(mix, stack(own_high, zeros)) + nn(mix, stack(own_low, zeros))
    other = nn(mix, stack(zeros, other_high)) + nn(mix, stack(zeros, other_low))
    own = own.astype(BF)
    other = other.astype(BF)
    out_ref[:, 0:32, :] = own[:, 0:128].reshape(CHIPS, 32, 128)
    out_ref[:, 32:64, :] = other[:, 0:128].reshape(CHIPS, 32, 128)
    out_ref[:, 64:96, 0:64] = own[:, 128:192].reshape(CHIPS, 32, 64)
    out_ref[:, 64:96, 64:128] = other[:, 128:192].reshape(CHIPS, 32, 64)


def spread(own, other, mix):
    whole = pl.BlockSpec(memory_space=pltpu.VMEM)
    return pl.pallas_call(
        spread_kernel,
        out_shape=jax.ShapeDtypeStruct((CHIPS, 96, 128), BF),
        in_specs=[whole] * 3,
        name="spread",
    )(own, other, mix)


def total_kernel(pieces_ref, *refs):
    out_ref = refs[-1]
    total = pieces_ref[0].astype(F32)
    for chip in range(1, CHIPS):
        total = total + pieces_ref[chip].astype(F32)
    out_ref[...] = total.astype(BF)


def sum_pieces(pieces, *after):
    return pl.pallas_call(
        total_kernel,
        out_shape=jax.ShapeDtypeStruct((64, 128), BF),
        in_specs=[pl.BlockSpec(memory_space=pltpu.VMEM)]
        + [pl.BlockSpec(memory_space=pl.ANY)] * len(after),
        name="sum_pieces",
    )(near(pieces), *after)


def assemble(place_ref, mine_ref, theirs_ref, out_refs):
    for piece in range(27):
        dx = (place_ref[2] - piece // 8 + 4) % 4
        dz = (place_ref[3] - piece % 8 + 8) % 8
        out_ref = out_refs[(piece % 9) // 3]
        rows = slice(64 * (piece % 3), 64 * (piece % 3) + 64)
        mine = mine_ref[dx, dz].astype(F32)
        theirs = theirs_ref[dx, dz].astype(F32)
        low = place_ref[1] == 0
        tile = 128 * (piece // 9)
        out_ref[rows, tile : tile + 128] = jnp.where(low, mine, theirs)
        out_ref[rows, 384 + tile : 512 + tile] = jnp.where(low, theirs, mine)


def scatter_kernel(
    place_ref, index_ref, rows_ref, mine_ref, theirs_ref,
    out_ref, wq_ref, wk_ref, wv_ref, turned_ref,
):
    step = pl.program_id(0)

    @pl.when(step == 0)
    def _():
        assemble(place_ref, mine_ref, theirs_ref, (wq_ref, wk_ref, wv_ref))
        for g in range(8):
            chips = slice(4 * g, 4 * g + 4)
            first = rows_ref[chips, 0:32, :].reshape(128, 128).astype(F32).T.astype(BF)
            second = rows_ref[chips, 32:64, :].reshape(128, 128).astype(F32).T.astype(BF)
            both = rows_ref[chips, 64:96, :].reshape(128, 128).astype(F32).T.astype(BF)
            lanes = slice(256 * g, 256 * g + 128)
            more = slice(256 * g + 128, 256 * g + 256)
            turned_ref[0:128, lanes] = first
            turned_ref[128:192, lanes] = both[0:64]
            turned_ref[0:128, more] = second
            turned_ref[128:192, more] = both[64:128]

    row = lax.broadcasted_iota(jnp.int32, (256, 2048), 0) + 256 * step
    select = jnp.where(row == index_ref[...], 1.0, 0.0).astype(BF)
    out_ref[...] = nt(turned_ref[...], select)


def scatter_rows(place, index, rows, mine, theirs):
    weight = jax.ShapeDtypeStruct((192, 768), F32)
    weight_block = pl.BlockSpec((192, 768), lambda i: (0, 0))
    whole = pl.BlockSpec(memory_space=pltpu.VMEM)
    return pl.pallas_call(
        scatter_kernel,
        out_shape=(jax.ShapeDtypeStruct((192, 2048), F32), weight, weight, weight),
        grid=(8,),
        in_specs=[
            pl.BlockSpec(memory_space=pltpu.SMEM),
            pl.BlockSpec((1, 2048), lambda i: (0, 0)),
            whole,
            whole,
            whole,
        ],
        out_specs=(
            pl.BlockSpec((192, 256), lambda i: (0, i)), weight_block, weight_block, weight_block
        ),
        scratch_shapes=[pltpu.VMEM((192, 2048), BF)],
        compiler_params=pltpu.CompilerParams(vmem_limit_bytes=VMEM_LIMIT),
        name="scatter_rows",
    )(place, index, near(rows), near(mine), near(theirs))


def layer(tokens, w_query, w_key, w_value, grad_out, owned_cls, send_rows, neigh_slot, neigh_count):
    node = lax.axis_index("nodes")
    core = node % 2
    place = jnp.stack([lax.axis_index("mp"), core, node // 16, node // 2 % 8]).astype(jnp.int32)

    asked = send_rows.reshape(8, 4, 2, 32)
    asked = jnp.where(core == 0, asked, asked[:, :, ::-1])
    index = asked.transpose(0, 2, 1, 3).reshape(8, 1, 256)
    sent = gather_rows(index, owned_cls)

    slots = neigh_slot.reshape(64, 32)
    counts = neigh_count.reshape(64, 1)
    position = lax.broadcasted_iota(jnp.int32, (64, 32), 1)
    slots = jnp.where(position < counts, slots, -1)
    all_slots = jnp.concatenate([slots, core_swap(slots)], axis=0)
    here = (all_slots >= 0) & (((all_slots >> 5) & 1) == core)
    keys = jnp.where(here, (all_slots >> 6) * 32 + (all_slots & 31), -1).T
    mix = make_mixing(keys)

    heads = grad_out.transpose(1, 0, 2).reshape(3, 2048, HD)
    wk4 = w_key.reshape(192, 4, 192).transpose(1, 0, 2)
    wv4 = w_value.reshape(192, 4, 192).transpose(1, 0, 2)

    flat = tokens.reshape(2048, 768)
    q, k, v = project(flat, w_query, w_key, w_value)

    fetched = chip_exchange(sent)
    own_part, other_part = mix_rows(fetched, mix, q, k, v, heads, wk4, wv4)
    divisor = counts.astype(F32)
    local = ((own_part + core_swap(other_part)) / divisor).astype(BF)
    virtual = lax.all_gather(local, "mp", axis=1, tiled=True)

    ctx, keep, give, vg0, vg1, vg2, vg3 = attend(
        place, flat, q, k, v, heads, virtual, w_key, w_value, wk4, wv4
    )
    context = ctx.reshape(3, 32, 4096).transpose(1, 0, 2)

    around = lambda x, d: lax.ppermute(x, "mp", [(i, (i + d) % 4) for i in range(4)])
    moved = [around(vg, d + 1) for d, vg in enumerate((vg1, vg2, vg3))]
    half = (keep + core_swap(give).astype(F32)).astype(BF)
    pieces = chip_exchange(half.reshape(CHIPS, 64, 128))

    shared = (vg0 + moved[0].astype(F32) + moved[1].astype(F32) + moved[2].astype(F32)) / divisor
    outgoing = spread(shared, core_swap(shared), mix)
    total = sum_pieces(pieces, outgoing, context.transpose(1, 0, 2))
    arrived = chip_exchange(outgoing)
    close = jnp.stack([total] + [along(total, 0, d) for d in range(1, 4)])
    across = along(close, 0, 4)
    row = jnp.concatenate([close, across], axis=0)
    mine = jnp.stack([row] + [along(row, d, 0) for d in range(1, 4)])
    theirs = core_swap(mine)
    grad_cls, grad_query, grad_key, grad_value = scatter_rows(
        place, index.reshape(1, 2048), arrived, mine, theirs
    )
    return (context, grad_query, grad_key, grad_value, grad_cls)


def solution(mesh):
    in_specs = (
        P("nodes", None, None),
        P("mp", None),
        P("mp", None),
        P("mp", None),
        P("nodes", "mp", None),
        P("mp", "nodes"),
        P("nodes", None, None),
        P("nodes", None, None),
        P("nodes", None),
    )
    out_specs = (
        P("nodes", "mp", None),
        P("mp", None),
        P("mp", None),
        P("mp", None),
        P("mp", "nodes"),
    )
    return jax.shard_map(layer, mesh=mesh, in_specs=in_specs, out_specs=out_specs, check_vma=False)
```
